1024 devices in a mesh: mem: 8 (over z), lev: 32 (over y_lo, x), row: 4 (over y_hi, core).
Axes of the slice: x: 8, y: 8 (y_hi: 2, y_lo: 4; y = y_hi * 4 + y_lo), z: 8, core: 2. Of those that a mesh axis runs over, the one named last changes fastest.
Arguments:
- control: bfloat16 [16, 64, 128, 256], P('mem', 'lev', 'row'), may hold values from -6 to 6
- members: bfloat16 [16, 64, 32768], P('mem', None, ('row', 'lev')), may hold values from -3 to 3
- east_coef: float32 [64, 128, 256], P('lev', 'row'), may hold values from 0.12 to 0.245
- south_coef: float32 [64, 128, 256], P('lev', 'row'), may hold values from 0.12 to 0.245
- innovation: float32 [64, 32768], P(None, ('row', 'lev')), may hold values from -6 to 6
- huber_class: int32 [64, 32768], P(None, ('row', 'lev')), may hold values 0 or 1
- band: float32 [7, 64], replicated, may hold values from -0.4 to 0.4
- level_group_index: int32 [64], replicated, may hold values from 0 to 16, never falling along the last dimension, each value on 1 to 8 neighbouring positions
Outputs:
- gradient: float32 [16, 64, 128, 256], P('mem', 'lev', 'row')
The draws below stay inside these ranges and needn't reach their ends.
Inputs may be any that keep to these rules, and one draw needn't show every extreme that they name: `level_group_index`: never falls along the levels; every group 0 to 16 holds 1 to 8 consecutive levels.
All inputs are finite; a program needn't handle non-finite values. No bound on the sum of `huber_class` on one device may be relied on, other than what follows from the above.
Results may differ from the reference program's by a relative error of at most 0.0003.
Values sent between devices are 32-bit elements; how exact they have to be, the bound alone decides.
A program may use at most 32 MiB of HBM per device.

```python
import math
import jax
import jax.numpy as jnp
import numpy as np
from jax import lax

LON = 256
PASSES = 8
MEMBERS = 16
LEV = 64
LAT = 128
CELLS = 32768
GROUPS = 17
GROUP_MOST = 8


def draw_control(key, part):
    cell_key = jax.random.fold_in(key, 11)
    zonal_key = jax.random.fold_in(key, 12)
    cell = 0.7 * jnp.clip(jax.random.normal(cell_key, (MEMBERS, LEV, LAT, LON), jnp.float32), -4.0, 4.0)
    zonal = 0.7 * jnp.clip(jax.random.normal(zonal_key, (MEMBERS, LEV, LAT, 1), jnp.float32), -4.0, 4.0)
    field = cell + zonal
    return field.astype(jnp.bfloat16)


def set_ends(entries, key, low, top_value):
    longest = entries.shape.index(max(entries.shape))
    spots = []
    for shift in (0, 1):
        where = [jax.random.randint(jax.random.fold_in(key, axis), (), 0, length) for axis, length in enumerate(entries.shape)]
        where[longest] = (where[longest] + shift) % entries.shape[longest]
        spots.append(tuple(where))
    return entries.at[spots[0]].set(low).at[spots[1]].set(top_value)


def level_of(stream_key, dims, split, low, top_value):
    def one(axis_at, parts):
        heights = jax.random.uniform(jax.random.fold_in(jax.random.fold_in(stream_key, 6), axis_at), (parts,), jnp.float32, low / len(split), top_value / len(split))
        return jnp.repeat(jnp.exp(heights), dims[axis_at] // parts).reshape((-1,) + (1,) * (len(dims) - axis_at - 1))

    loudness = one(*split[0])
    for cut in split[1:]:
        loudness = loudness * one(*cut)
    return loudness


def split_up(amount, total, reach, lean):
    weights = [(1 << 20) // math.isqrt(grade ** lean) + 1 for grade in range(2, amount + 1)]
    spare, given = total - reach - (amount - 1), [1] * (amount - 1)
    while spare > 0:
        free = [i for i in range(amount - 1) if given[i] < reach]
        mass, budget = sum([weights[i] for i in free]), spare
        for i in free:
            extra = min(reach - given[i], max(1, budget * weights[i] // mass), spare)
            given[i] = given[i] + extra
            spare = spare - extra
    return np.array([reach] + given)


def ragged(stream_key, amount, total, limit, lean):
    if amount == 2:
        one = jax.random.randint(stream_key, (), max(1, total - limit), min(limit, total - 1) + 1)
        return jnp.stack([one, total - one])
    lengths = jnp.asarray(split_up(amount, total, limit, lean), jnp.int32)
    twos = (amount - 1) // 2
    giver, receiver = lengths[1:1 + 2 * twos:2], lengths[2:2 + 2 * twos:2]
    margin = jnp.minimum(giver - 1, limit - receiver)
    moved = jax.random.randint(jax.random.fold_in(stream_key, 1), (twos,), 0, 1 << 20) % (margin + 1)
    lengths = lengths.at[1:1 + 2 * twos:2].set(giver - moved).at[2:2 + 2 * twos:2].set(receiver + moved)
    return lengths[jax.random.permutation(jax.random.fold_in(stream_key, 2), amount)]


def noise(own_key, dims, scale, bound, shards=(), held_as=jnp.bfloat16):
    factor_of = level_of(own_key, dims, shards, -0.22, 0.18) if shards else 1.0
    result = jax.random.normal(own_key, dims, jnp.float32) * scale * factor_of
    return jnp.minimum(jnp.maximum(result, -bound), bound).astype(held_as)


def setup_inputs(seed: int = 0) -> dict:
    streams_of = jax.random.split(jax.random.key(seed), 9)
    return {
        "control": draw_control(jax.random.fold_in(streams_of[8], 71), 0),
        "members": noise(streams_of[1], (MEMBERS, LEV, CELLS), 0.5, 3.0, ((0, 8), (2, 128))),
        "east_coef": jnp.clip(jnp.exp(math.log(0.245) - 0.7137665 * jax.random.uniform(streams_of[2], (LEV, LAT, LON), jnp.float32) ** level_of(streams_of[2], (LEV, LAT, LON), ((0, 32), (1, 4)), -0.2, 0.2)), 0.12, 0.245),
        "south_coef": jnp.clip(jnp.exp(math.log(0.245) - 0.7137665 * jax.random.uniform(streams_of[3], (LEV, LAT, LON), jnp.float32) ** level_of(streams_of[3], (LEV, LAT, LON), ((0, 32), (1, 4)), -0.2, 0.2)), 0.12, 0.245),
        "innovation": noise(streams_of[4], (LEV, CELLS), 1.0, 6.0, ((1, 128),), jnp.float32),
        "huber_class": set_ends((jax.random.randint(streams_of[5], (LEV, CELLS), 0, 2) < 1).astype(jnp.int32), jax.random.fold_in(streams_of[5], 1), 0, 1),
        "band": jnp.clip(jax.random.uniform(streams_of[6], (7, LEV), jnp.float32, -0.4, 0.4), -0.4, 0.4),
        "level_group_index": jnp.searchsorted(jnp.cumsum(ragged(streams_of[7], GROUPS, LEV, GROUP_MOST, 2)), jnp.arange(LEV), side="right").astype(jnp.int32),
    }


HUBER = 1.0


def smooth_rows(extended, east, south):
    center = extended[..., 1:-1, :]
    flux_x = east * (jnp.roll(center, -1, axis=-1) - center)
    flux_y = south * (extended[..., 1:, :] - extended[..., :-1, :])
    return center + flux_x - jnp.roll(flux_x, 1, axis=-1) + flux_y[..., 1:, :] - flux_y[..., :-1, :]


def pad_rows(field):
    widths = [(0, 0)] * (field.ndim - 2) + [(1, 1), (0, 0)]
    return jnp.pad(field, widths)


def vertical_level_matrix(band, level_group_index):
    count = band.shape[1]
    rows = jnp.arange(count)[:, None]
    cols = jnp.arange(count)[None, :]
    same = level_group_index[:, None] == level_group_index[None, :]
    matrix = jnp.zeros((count, count), jnp.float32)
    for offset in range(7):
        coef = band[offset] + (1.0 if offset == 3 else 0.0)
        hit = (cols == rows + offset - 3) & same
        matrix = matrix + jnp.where(hit, coef[:, None], jnp.float32(0.0))
    return matrix


def huber_weight(residual, classes):
    scale = HUBER / jnp.maximum(jnp.abs(residual), HUBER)
    return jnp.where(classes == 1, scale, jnp.float32(1.0)) * residual


def reference(control, members, east_coef, south_coef, innovation, huber_class, band, level_group_index):
    zero_row = jnp.zeros((LEV, 1, LON), jnp.float32)
    south_faces = jnp.concatenate([south_coef, zero_row], axis=1)
    vertical_matrix = vertical_level_matrix(band, level_group_index)

    def diffuse(field):
        for step in range(PASSES):
            field = smooth_rows(pad_rows(field), east_coef, south_faces)
        return field

    def forward_member(carry, pair):
        ctrl, ensemble_states = pair
        smoothed_field = diffuse(ctrl.astype(jnp.float32)).reshape(LEV, LAT * LON)
        filtered_field = jnp.dot(vertical_matrix, smoothed_field, precision=lax.Precision.HIGHEST)
        return carry + ensemble_states.astype(jnp.float32) * filtered_field, None

    increment, unused = lax.scan(forward_member, jnp.zeros((LEV, LAT * LON), jnp.float32), (control, members))
    weighted_field = huber_weight(increment - innovation, huber_class)

    def backward_member(pair):
        ctrl, ensemble_states = pair
        lifted_field = jnp.dot(vertical_matrix.T, ensemble_states.astype(jnp.float32) * weighted_field, precision=lax.Precision.HIGHEST)
        return ctrl.astype(jnp.float32) + diffuse(lifted_field.reshape(LEV, LAT, LON))

    return lax.map(backward_member, (control, members))
```

```python
import functools

import jax
import jax.numpy as jnp
from jax import lax
from jax.experimental import pallas as pl
from jax.experimental.pallas import tpu as pltpu
from jax.sharding import PartitionSpec as P

PASSES = 8
HUBER = 1.0
MESH = pl.DeviceIdType.MESH
F32 = jnp.float32

LANES = 128
SUB = 8
LATS = 32
HALO = 8
FIRST = HALO + 1
ROWS = LATS + 2 * FIRST
LEVS = 32
MEMS = 8
BLOCKS = 4
CHUNK = 16


def tiles(start, count):
    return pl.ds(pl.multiple_of(SUB * start, SUB), SUB * count)


def sublane(member, level, half):
    return 4 * half + 2 * member + level


def next_longitude(x, lane):
    turned = pltpu.roll(x, LANES - 1, 2)
    return jnp.where(lane == LANES - 1, pltpu.roll(turned, 4, 1), turned)


def previous_longitude(x, lane):
    turned = pltpu.roll(x, 1, 2)
    return jnp.where(lane == 0, pltpu.roll(turned, 4, 1), turned)


def diffuse(field, other, east, south, keep_lower):
    lane = lax.broadcasted_iota(jnp.int32, (8, SUB, LANES), 2)

    def rows_of(ref, start):
        return ref[tiles(start, 8), :].reshape(8, SUB, LANES)

    def one_pass(source, target):
        for chunk in range(LATS // 8 + 2):
            start = 1 + 8 * chunk
            center = rows_of(source, start)
            flux_x = rows_of(east, start) * (next_longitude(center, lane) - center)
            flux_in = rows_of(south, start) * (center - rows_of(source, start - 1))
            flux_out = rows_of(south, start + 1) * (rows_of(source, start + 1) - center)
            result = center + flux_x - previous_longitude(flux_x, lane) + flux_out - flux_in
            if chunk == 0:
                result = result * keep_lower
            target[tiles(start, 8), :] = result.reshape(8 * SUB, LANES)

    @pl.loop(0, PASSES // 2)
    def _(step):
        one_pass(field, other)
        one_pass(other, field)


def vertical_columns(band_ref, group_ref, out_ref):
    band = band_ref[...]
    group = group_ref[...]
    group = jnp.concatenate([group, group], axis=1)
    coefs = []
    for offset in range(-3, 4):
        coef = band[offset + 3 : offset + 4, :] + (1.0 if offset == 0 else 0.0)
        coef = jnp.concatenate([coef, coef], axis=1)
        ahead = group if offset == 0 else pltpu.roll(group, (-offset) % LANES, 1)
        coef = jnp.where(ahead == group, coef, 0.0)
        coefs.append(jnp.concatenate([coef, coef], axis=1))

    @pl.loop(0, 8)
    def _(part):
        shape = (32, 256)
        row = lax.broadcasted_iota(jnp.int32, shape, 0) + 32 * part
        col = lax.broadcasted_iota(jnp.int32, shape, 1)
        half, member, level = (row // 4) % 2, (row // 2) % 2, row % 2
        apart = 2 * (row // SUB) + level + 1024 * (2 * member + half) - col % 64 - 1024 * (col // 64)
        total = jnp.zeros(shape, F32)
        for offset in range(-3, 4):
            total = jnp.where(apart == offset, coefs[offset + 3], total)
        out_ref[pl.ds(pl.multiple_of(32 * part, 32), 32), :] = total


def kernel(
    control_hbm, members_hbm, east_hbm, south_hbm, innovation_hbm, huber_hbm, band_ref, group_ref,
    out_hbm,
    control, members, east_in, south_in, innovation, huber, out,
    east, south, field, other, lifted_field, east_edge, south_edge,
    gathered, lift, lower_matrix, upper_matrix,
    part_sums, parts, weighted, weighted_all,
    local_sems, edge_send, edge_recv, fwd_sems, sum_sems, share_sems, back_send, back_recv,
):
    m, l, r = lax.axis_index("mem"), lax.axis_index("lev"), lax.axis_index("row")
    has_lower = (r + BLOCKS - 1) // BLOCKS
    has_upper = 1 - (r + 1) // BLOCKS
    low_edge = 1 - (l + LEVS - HALO) // LEVS
    high_edge = (l + HALO) // LEVS

    def remote(source, target, send, recv, **where):
        return pltpu.make_async_remote_copy(
            src_ref=source, dst_ref=target, send_sem=send, recv_sem=recv,
            device_id=where, device_id_type=MESH,
        )

    barrier = pltpu.get_barrier_semaphore()

    def greet(**where):
        pl.semaphore_signal(barrier, inc=1, device_id=where, device_id_type=MESH)

    @pl.when(r > 0)
    def _():
        greet(row=r - 1)

    @pl.when(r < BLOCKS - 1)
    def _():
        greet(row=r + 1)

    @pl.loop(1, LEVS)
    def _(i):
        greet(lev=lax.rem(l + i, LEVS))

    @pl.loop(1, MEMS)
    def _(i):
        greet(mem=lax.rem(m + i, MEMS))

    @pl.when(r > 0)
    def _():
        @pl.loop(0, HALO)
        def _(i):
            greet(lev=LEVS - HALO + i, row=r - 1)

    @pl.when(r < BLOCKS - 1)
    def _():
        @pl.loop(0, HALO)
        def _(i):
            greet(lev=i, row=r + 1)

    mine = (
        pl.ds(pl.multiple_of(CHUNK * lax.rem(m, 4), CHUNK), CHUNK),
        pl.ds(pl.multiple_of(LANES * (m // 4), LANES), LANES),
    )
    loads = [
        pltpu.make_async_copy(source, target, local_sems.at[i])
        for i, (source, target) in enumerate([
            (control_hbm, control), (east_hbm, east_in), (south_hbm, south_in),
            (members_hbm, members),
            (innovation_hbm.at[mine[0], mine[1]], innovation),
            (huber_hbm.at[mine[0], mine[1]], huber),
        ])
    ]
    for load in loads:
        load.start()

    blank = jnp.zeros((HALO * SUB, LANES), F32)
    for ref in (east, south, field, other, lifted_field):
        ref[tiles(0, 1), :] = blank[:SUB]
        ref[tiles(ROWS - 1, 1), :] = blank[:SUB]

    @pl.when(r == 0)
    def _():
        for ref in (east, south, field, lifted_field):
            ref[tiles(1, HALO), :] = blank

    @pl.when(r == BLOCKS - 1)
    def _():
        for ref in (east, south, field, lifted_field):
            ref[tiles(FIRST + LATS, HALO), :] = blank

    loads[0].wait()
    for member in range(2):
        for level in range(2):
            own = control[member, level].astype(F32)
            for half in range(2):
                field[pl.ds(SUB * FIRST + sublane(member, level, half), LATS, stride=SUB), :] = own[
                    :, half * LANES : (half + 1) * LANES
                ]
    loads[1].wait()
    loads[2].wait()

    pl.semaphore_wait(
        barrier,
        LEVS - 1 + MEMS - 1 + has_lower + has_upper
        + LEVS * (low_edge * has_lower + high_edge * has_upper),
    )

    def edge_copies(side, row):
        edge = slice(0, HALO) if side == 0 else slice(LATS - HALO, LATS)
        first = FIRST if side == 0 else FIRST + LATS - HALO
        landing = FIRST + LATS if side == 0 else 1
        return [
            remote(field.at[tiles(first, HALO), :], field.at[tiles(landing, HALO), :],
                   edge_send.at[side, 0], edge_recv.at[side, 0], row=row),
            remote(east_in.at[:, edge, :], east_edge.at[side],
                   edge_send.at[side, 1], edge_recv.at[side, 1], row=row),
            remote(south_in.at[:, edge, :], south_edge.at[side],
                   edge_send.at[side, 2], edge_recv.at[side, 2], row=row),
        ]

    @pl.when(r > 0)
    def _():
        for copy in edge_copies(0, r - 1):
            copy.start()

    @pl.when(r < BLOCKS - 1)
    def _():
        for copy in edge_copies(1, r + 1):
            copy.start()

    def place(target, value, level, first, count):
        for half in range(2):
            for member in range(2):
                target[pl.ds(SUB * first + sublane(member, level, half), count, stride=SUB), :] = value[
                    :, half * LANES : (half + 1) * LANES
                ]

    for level in range(2):
        place(east, east_in[level], level, FIRST, LATS)
        place(south, south_in[level], level, FIRST, LATS)
    vertical_columns(band_ref, group_ref, upper_matrix)
    lower_matrix[...] = upper_matrix[...].T
    for load in loads[3:]:
        load.wait()

    def take_edge(side, first):
        for copy in edge_copies(side, r):
            copy.wait_recv()
        for level in range(2):
            place(east, east_edge[side, level], level, first, HALO)
            place(south, south_edge[side, level], level, first, HALO)

    @pl.when(r < BLOCKS - 1)
    def _():
        take_edge(0, FIRST + LATS)

    @pl.when(r > 0)
    def _():
        take_edge(1, 1)

    @pl.when(r > 0)
    def _():
        for copy in edge_copies(0, r - 1):
            copy.wait_send()

    @pl.when(r < BLOCKS - 1)
    def _():
        for copy in edge_copies(1, r + 1):
            copy.wait_send()

    keep_lower = has_lower.astype(F32)
    diffuse(field, other, east, south, keep_lower)

    @pl.loop(1, LEVS)
    def _(i):
        peer = lax.rem(l + i, LEVS)
        remote(field.at[tiles(FIRST + peer, 1), :], gathered.at[tiles(l, 1), :],
               fwd_sems.at[0], fwd_sems.at[1], lev=peer).start()

    gathered[tiles(l, 1), :] = field[tiles(FIRST + l, 1), :]
    everyone = remote(field.at[tiles(FIRST, LEVS - 1), :], gathered.at[tiles(0, LEVS - 1), :],
                      fwd_sems.at[0], fwd_sems.at[1], lev=l)
    everyone.wait_recv()

    filtered = jnp.dot(lower_matrix[...], gathered[...], precision=lax.Precision.HIGHEST,
                       preferred_element_type=F32)

    def member_columns(member, half):
        return members[member, :, half * LANES : (half + 1) * LANES].astype(F32)

    for half in range(2):
        term = sum(
            member_columns(member, half) * filtered[64 * (2 * member + half) : 64 * (2 * member + half + 1)]
            for member in range(2)
        )
        for quarter in range(4):
            part_sums[4 * half + quarter] = term[CHUNK * quarter : CHUNK * (quarter + 1)]

    @pl.loop(1, MEMS)
    def _(i):
        peer = lax.rem(m + i, MEMS)
        remote(part_sums.at[peer], parts.at[m], sum_sems.at[0], sum_sems.at[1], mem=peer).start()

    parts[m] = part_sums[m]
    all_parts = remote(part_sums.at[pl.ds(0, MEMS - 1)], parts.at[pl.ds(0, MEMS - 1)],
                       sum_sems.at[0], sum_sems.at[1], mem=m)
    all_parts.wait_recv()
    increment = parts[0]
    for i in range(1, MEMS):
        increment = increment + parts[i]
    residual = increment - innovation[...]
    scale = HUBER / jnp.maximum(jnp.abs(residual), HUBER)
    weighted[...] = jnp.where(huber[...] == 1, scale, 1.0) * residual

    @pl.loop(1, MEMS)
    def _(i):
        peer = lax.rem(m + i, MEMS)
        remote(weighted, weighted_all.at[m], share_sems.at[0], share_sems.at[1], mem=peer).start()

    weighted_all[m] = weighted[...]
    all_shares = remote(weighted_all.at[pl.ds(0, MEMS - 1)], weighted_all.at[pl.ds(0, MEMS - 1)],
                        share_sems.at[0], share_sems.at[1], mem=m)
    all_shares.wait_recv()

    columns = weighted_all[...].reshape(2, 64, LANES)
    adjoint = jnp.concatenate(
        [member_columns(member, half) * columns[half] for member in range(2) for half in range(2)], axis=0
    )
    lift[...] = jnp.dot(upper_matrix[...], adjoint, precision=lax.Precision.HIGHEST,
                        preferred_element_type=F32)

    def back(peer, landing, way, **where):
        return remote(lift.at[tiles(peer, 1), :], lifted_field.at[tiles(landing, 1), :],
                      back_send.at[way], back_recv.at[way], lev=peer, **where)

    @pl.when(low_edge * has_lower == 1)
    def _():
        @pl.loop(0, LEVS)
        def _(i):
            back(lax.rem(l + i, LEVS), FIRST + LATS + l, 1, row=r - 1).start()

    @pl.when(high_edge * has_upper == 1)
    def _():
        @pl.loop(0, LEVS)
        def _(i):
            back(lax.rem(l + i, LEVS), 1 + l - (LEVS - HALO), 2, row=r + 1).start()

    @pl.loop(1, LEVS)
    def _(i):
        back(lax.rem(l + i, LEVS), FIRST + l, 0).start()

    lifted_field[tiles(FIRST + l, 1), :] = lift[tiles(l, 1), :]

    def batch(way, count):
        return remote(lift.at[tiles(0, count), :], lift.at[tiles(0, count), :],
                      back_send.at[way], back_recv.at[way], lev=l)

    batch(0, LEVS - 1).wait_recv()

    @pl.when(r < BLOCKS - 1)
    def _():
        batch(1, HALO).wait_recv()

    @pl.when(r > 0)
    def _():
        batch(2, HALO).wait_recv()

    diffuse(lifted_field, other, east, south, keep_lower)

    for member in range(2):
        for level in range(2):
            for half in range(2):
                lanes = slice(half * LANES, (half + 1) * LANES)
                smooth = lifted_field[
                    pl.ds(SUB * FIRST + sublane(member, level, half), LATS, stride=SUB), :
                ]
                out[member, level, :, lanes] = control[member, level, :, lanes].astype(F32) + smooth

    store = pltpu.make_async_copy(out, out_hbm, local_sems.at[0])
    store.start()
    everyone.wait_send()
    all_parts.wait_send()
    all_shares.wait_send()
    batch(0, LEVS - 1).wait_send()

    @pl.when(low_edge * has_lower == 1)
    def _():
        batch(1, LEVS).wait_send()

    @pl.when(high_edge * has_upper == 1)
    def _():
        batch(2, LEVS).wait_send()

    store.wait()


def per_device(
    control, members, east_coef, south_coef, innovation, huber_class, band, level_group_index
):
    hbm = pl.BlockSpec(memory_space=pl.ANY)
    vmem = pl.BlockSpec(memory_space=pltpu.VMEM)
    dma = pltpu.SemaphoreType.DMA
    return pl.pallas_call(
        kernel,
        out_shape=jax.ShapeDtypeStruct(control.shape, F32),
        in_specs=[hbm] * 6 + [vmem] * 2,
        out_specs=hbm,
        scratch_shapes=[
            pltpu.VMEM(control.shape, jnp.bfloat16),
            pltpu.VMEM(members.shape, jnp.bfloat16),
            pltpu.VMEM(east_coef.shape, F32),
            pltpu.VMEM(south_coef.shape, F32),
            pltpu.VMEM((CHUNK, LANES), F32),
            pltpu.VMEM((CHUNK, LANES), jnp.int32),
            pltpu.VMEM(control.shape, F32),
            pltpu.VMEM((SUB * ROWS, LANES), F32),
            pltpu.VMEM((SUB * ROWS, LANES), F32),
            pltpu.VMEM((SUB * ROWS, LANES), F32),
            pltpu.VMEM((SUB * ROWS, LANES), F32),
            pltpu.VMEM((SUB * ROWS, LANES), F32),
            pltpu.VMEM((2, 2, HALO, 2 * LANES), F32),
            pltpu.VMEM((2, 2, HALO, 2 * LANES), F32),
            pltpu.VMEM((SUB * LEVS, LANES), F32),
            pltpu.VMEM((SUB * LEVS, LANES), F32),
            pltpu.VMEM((256, 256), F32),
            pltpu.VMEM((256, 256), F32),
            pltpu.VMEM((MEMS, CHUNK, LANES), F32),
            pltpu.VMEM((MEMS, CHUNK, LANES), F32),
            pltpu.VMEM((CHUNK, LANES), F32),
            pltpu.VMEM((MEMS, CHUNK, LANES), F32),
            dma((6,)),
            dma((2, 3)),
            dma((2, 3)),
            dma((2,)),
            dma((2,)),
            dma((2,)),
            dma((3,)),
            dma((3,)),
        ],
        compiler_params=pltpu.CompilerParams(collective_id=0, has_side_effects=True),
        name="hybrid_gradient",
    )(
        control, members, east_coef, south_coef, innovation, huber_class, band,
        level_group_index.reshape(1, -1),
    )


def solution(mesh):
    placed = (
        P("mem", "lev", "row", None),
        P("mem", None, ("row", "lev")),
        P("lev", "row", None),
        P("lev", "row", None),
        P(None, ("row", "lev")),
        P(None, ("row", "lev")),
        P(),
        P(),
    )
    return jax.shard_map(
        per_device,
        mesh=mesh,
        in_specs=placed,
        out_specs=P("mem", "lev", "row", None),
        check_vma=False,
    )
```

```python
import jax
import jax.numpy as jnp
from jax import lax
from jax.experimental import pallas as pl
from jax.experimental.pallas import tpu as pltpu
from jax.sharding import PartitionSpec as P

PASSES = 8
HUBER = 1.0
MESH = pl.DeviceIdType.MESH
F32 = jnp.float32

LANES = 128
SUB = 8
LATS = 32
HALO = 8
FIRST = HALO
ROWS = LATS + 2 * HALO
LEVS = 32
WIDE = 8
MEMS = 8
ROOT = MEMS - 1
BLOCKS = 4
FAR_FIRST = (4, 3, 5, 2, 6, 1, 7, 0)


def tiles(start, count):
    if isinstance(start, int):
        return pl.ds(SUB * start, SUB * count)
    return pl.ds(pl.multiple_of(SUB * start, SUB), SUB * count)


def sublane(member, level, half):
    return 4 * half + 2 * member + level


def next_longitude(x, lane):
    turned = pltpu.roll(x, LANES - 1, 2)
    return jnp.where(lane == LANES - 1, pltpu.roll(turned, 4, 1), turned)


def previous_longitude(x, lane):
    turned = pltpu.roll(x, 1, 2)
    return jnp.where(lane == 0, pltpu.roll(turned, 4, 1), turned)


def lane_index():
    return lax.broadcasted_iota(jnp.int32, (8, SUB, LANES), 2)


def one_pass(fields, coefs, step, start):
    east, west, south = coefs
    lane = lane_index()

    def field(row):
        return fields[step - 1, tiles(row, 8), :].reshape(8, SUB, LANES)

    def coef(ref, row):
        return ref[tiles(row, 8), :].reshape(8, SUB, LANES)

    center = field(start)
    flux_x = coef(east, start) * (next_longitude(center, lane) - center)
    flux_west = coef(west, start) * (center - previous_longitude(center, lane))
    flux_in = coef(south, start) * (center - field(start - 1))
    flux_out = coef(south, start + 1) * (field(start + 1) - center)
    return center + flux_x - flux_west + flux_out - flux_in


def diffuse_inside(fields, coefs):
    for step in range(1, PASSES + 1):
        starts = list(range(step, 24 - step, 8)) + [24 - step]
        for start in starts:
            result = one_pass(fields, coefs, step, FIRST + start)
            fields[step, tiles(FIRST + start, 8), :] = result.reshape(8 * SUB, LANES)


def diffuse_edges(fields, coefs, keep_lower):
    row = lax.broadcasted_iota(jnp.int32, (8, SUB, LANES), 0)

    @pl.loop(1, PASSES + 1)
    def _(step):
        low, high = FIRST - HALO + step, FIRST + LATS - step
        lower = one_pass(fields, coefs, step, low)
        upper = one_pass(fields, coefs, step, high)
        lower = lower * jnp.where(row + low >= FIRST, 1.0, keep_lower)
        fields[step, tiles(low, 8), :] = lower.reshape(8 * SUB, LANES)
        fields[step, tiles(high, 8), :] = upper.reshape(8 * SUB, LANES)


def vertical_columns(band_ref, group_ref, out_ref):
    band = band_ref[...]
    group = group_ref[...]
    group = jnp.concatenate([group, group], axis=1)
    coefs = []
    for offset in range(-3, 4):
        coef = band[offset + 3 : offset + 4, :] + (1.0 if offset == 0 else 0.0)
        coef = jnp.concatenate([coef, coef], axis=1)
        ahead = group if offset == 0 else pltpu.roll(group, (-offset) % LANES, 1)
        coef = jnp.where(ahead == group, coef, 0.0)
        coefs.append(jnp.concatenate([coef, coef], axis=1))

    @pl.loop(0, 8)
    def _(part):
        shape = (32, 256)
        row = lax.broadcasted_iota(jnp.int32, shape, 0) + 32 * part
        col = lax.broadcasted_iota(jnp.int32, shape, 1)
        half, member, level = (row // 4) % 2, (row // 2) % 2, row % 2
        apart = 2 * (row // SUB) + level + 1024 * (2 * member + half) - col % 64 - 1024 * (col // 64)
        total = jnp.zeros(shape, F32)
        for offset in range(-3, 4):
            total = jnp.where(apart == offset, coefs[offset + 3], total)
        out_ref[pl.ds(pl.multiple_of(32 * part, 32), 32), :] = total


def kernel(
    control_hbm, members_hbm, east_hbm, south_hbm, innovation_hbm, huber_hbm, band_hbm, group_hbm,
    out_hbm,
    control, members, east_in, south_in, innovation, huber, band, group, out,
    east, west, south, fields, back_fields, east_edge, south_edge,
    gathered, lift, relay, lower_matrix, upper_matrix,
    term, parts, share,
    local_sems, edge_send, edge_recv, fwd_sems, sum_sems, share_sems,
    back_sems, block_sems, relay_sems, lev_ready, mem_ready,
):
    m, l, r = lax.axis_index("mem"), lax.axis_index("lev"), lax.axis_index("row")
    along, across = l // WIDE, lax.rem(l, WIDE)
    has_lower = (r + BLOCKS - 1) // BLOCKS
    has_upper = 1 - (r + 1) // BLOCKS
    low_edge = 1 - (l + LEVS - HALO) // LEVS
    high_edge = (l + HALO) // LEVS
    from_low = low_edge * has_lower
    from_high = high_edge * has_upper
    coefs = (east, west, south)

    def leader(row):
        return 28 - 24 * (row // 2)

    is_leader = jnp.where(l == leader(r), 1, 0)
    is_root = m // ROOT

    def remote(source, target, send, recv, **where):
        return pltpu.make_async_remote_copy(
            src_ref=source, dst_ref=target, send_sem=send, recv_sem=recv,
            device_id=where, device_id_type=MESH,
        )

    barrier = pltpu.get_barrier_semaphore()

    def tell(sem, **where):
        pl.semaphore_signal(sem, inc=1, device_id=where, device_id_type=MESH)

    @pl.when(r > 0)
    def _():
        tell(barrier, row=r - 1)

    @pl.when(r < BLOCKS - 1)
    def _():
        tell(barrier, row=r + 1)

    @pl.when(is_leader == 0)
    def _():
        tell(barrier, lev=leader(r))

    @pl.when(is_root == 0)
    def _():
        tell(barrier, mem=ROOT)

    @pl.when(from_low == 1)
    def _():
        tell(barrier, lev=leader(r - 1), row=r - 1)

    @pl.when(from_high == 1)
    def _():
        tell(barrier, lev=leader(r + 1), row=r + 1)

    loads = [
        pltpu.make_async_copy(source, target, local_sems.at[i])
        for i, (source, target) in enumerate([
            (control_hbm, control), (east_hbm, east_in), (south_hbm, south_in),
            (band_hbm, band), (group_hbm, group),
            (members_hbm, members), (innovation_hbm, innovation), (huber_hbm, huber),
        ])
    ]
    for load in loads:
        load.start()

    blank = jnp.zeros((HALO * SUB, LANES), F32)
    halo_refs = (east, west, south, fields.at[0], back_fields.at[0])

    @pl.when(r == 0)
    def _():
        for ref in halo_refs:
            ref[tiles(0, HALO), :] = blank

    @pl.when(r == BLOCKS - 1)
    def _():
        for ref in halo_refs:
            ref[tiles(FIRST + LATS, HALO), :] = blank

    loads[0].wait()
    for member in range(2):
        for level in range(2):
            own = control[member, level].astype(F32)
            for half in range(2):
                fields[0, pl.ds(SUB * FIRST + sublane(member, level, half), LATS, stride=SUB), :] = own[
                    :, half * LANES : (half + 1) * LANES
                ]
    loads[1].wait()
    loads[2].wait()

    pl.semaphore_wait(
        barrier,
        has_lower + has_upper + is_root * (MEMS - 1)
        + is_leader * (LEVS - 1 + HALO * (has_lower + has_upper)),
    )

    def edge_copies(side, row):
        edge = slice(0, HALO) if side == 0 else slice(LATS - HALO, LATS)
        first = FIRST if side == 0 else FIRST + LATS - HALO
        landing = FIRST + LATS if side == 0 else 0
        return [
            remote(fields.at[0, tiles(first, HALO), :], fields.at[0, tiles(landing, HALO), :],
                   edge_send.at[side, 0], edge_recv.at[side, 0], row=row),
            remote(east_in.at[:, edge, :], east_edge.at[side],
                   edge_send.at[side, 1], edge_recv.at[side, 1], row=row),
            remote(south_in.at[:, edge, :], south_edge.at[side],
                   edge_send.at[side, 2], edge_recv.at[side, 2], row=row),
        ]

    @pl.when(r > 0)
    def _():
        for copy in edge_copies(0, r - 1):
            copy.start()

    @pl.when(r < BLOCKS - 1)
    def _():
        for copy in edge_copies(1, r + 1):
            copy.start()

    @pl.when(is_leader == 1)
    def _():
        @pl.loop(1, LEVS)
        def _(i):
            tell(lev_ready, lev=lax.rem(l + i, LEVS))

        @pl.when(r < BLOCKS - 1)
        def _():
            @pl.loop(0, HALO)
            def _(i):
                tell(lev_ready, lev=i, row=r + 1)

        @pl.when(r > 0)
        def _():
            @pl.loop(0, HALO)
            def _(i):
                tell(lev_ready, lev=LEVS - HALO + i, row=r - 1)

    @pl.when(is_root == 1)
    def _():
        @pl.loop(0, MEMS - 1)
        def _(i):
            tell(mem_ready, mem=i)

    def place(target, value, level, first, count):
        for half in range(2):
            for member in range(2):
                target[pl.ds(SUB * first + sublane(member, level, half), count, stride=SUB), :] = value[
                    :, half * LANES : (half + 1) * LANES
                ]

    def set_west(first):
        value = east[tiles(first, 8), :].reshape(8, SUB, LANES)
        west[tiles(first, 8), :] = previous_longitude(value, lane_index()).reshape(8 * SUB, LANES)

    for level in range(2):
        place(east, east_in[level], level, FIRST, LATS)
        place(south, south_in[level], level, FIRST, LATS)
    for first in range(FIRST, FIRST + LATS, 8):
        set_west(first)
    diffuse_inside(fields, coefs)

    pl.semaphore_wait(lev_ready, 1 - is_leader + from_low + from_high)

    def send_latitudes(rows):
        for apart in FAR_FIRST:
            for row in rows:
                peer = WIDE * row + lax.rem(across + apart, WIDE)

                def send(peer=peer):
                    remote(fields.at[PASSES, tiles(FIRST + peer, 1), :], gathered.at[tiles(l, 1), :],
                           fwd_sems.at[0], fwd_sems.at[1], lev=peer).start()

                if apart:
                    send()
                else:
                    pl.when(along != row)(send)

    send_latitudes((1, 2))

    for load in loads[3:]:
        load.wait()
    vertical_columns(band, group, upper_matrix)
    lower_matrix[...] = upper_matrix[...].T

    def take_edge(side, first):
        for copy in edge_copies(side, r):
            copy.wait_recv()
        for level in range(2):
            place(east, east_edge[side, level], level, first, HALO)
            place(south, south_edge[side, level], level, first, HALO)
        set_west(first)

    @pl.when(r < BLOCKS - 1)
    def _():
        take_edge(0, FIRST + LATS)

    @pl.when(r > 0)
    def _():
        take_edge(1, 0)

    keep_lower = has_lower.astype(F32)
    diffuse_edges(fields, coefs, keep_lower)
    send_latitudes((0, 3))

    gathered[tiles(l, 1), :] = fields[PASSES, tiles(FIRST + l, 1), :]
    everyone = remote(fields.at[PASSES, tiles(FIRST, LEVS - 1), :], gathered.at[tiles(0, LEVS - 1), :],
                      fwd_sems.at[0], fwd_sems.at[1], lev=l)
    everyone.wait_recv()

    filtered = jnp.dot(lower_matrix[...], gathered[...], precision=lax.Precision.HIGHEST,
                       preferred_element_type=F32)

    def member_columns(member, half):
        return members[member, :, half * LANES : (half + 1) * LANES].astype(F32)

    for half in range(2):
        term[half] = sum(
            member_columns(member, half) * filtered[64 * (2 * member + half) : 64 * (2 * member + half + 1)]
            for member in range(2)
        )

    def term_copy(half):
        return remote(term.at[half], parts.at[m, half], sum_sems.at[0, half], sum_sems.at[1, half], mem=ROOT)

    def share_copy(half, mem):
        return remote(share.at[half], share.at[half], share_sems.at[0, half], share_sems.at[1, half], mem=mem)

    def term_batch(half):
        return remote(parts.at[pl.ds(0, MEMS - 1), half], parts.at[pl.ds(0, MEMS - 1), half],
                      sum_sems.at[0, half], sum_sems.at[1, half], mem=ROOT)

    @pl.when(is_root == 0)
    def _():
        pl.semaphore_wait(mem_ready, 1)
        for half in range(2):
            term_copy(half).start()
        for half in range(2):
            share_copy(half, ROOT).wait_recv()

    @pl.when(is_root == 1)
    def _():
        for half in range(2):
            term_batch(half).wait_recv()
            increment = parts[0, half]
            for i in range(1, MEMS - 1):
                increment = increment + parts[i, half]
            increment = increment + term[half]
            lanes = slice(half * LANES, (half + 1) * LANES)
            residual = increment - innovation[:, lanes]
            scale = HUBER / jnp.maximum(jnp.abs(residual), HUBER)
            share[half] = jnp.where(huber[:, lanes] == 1, scale, 1.0) * residual
            for mem in (0, 6):
                share_copy(half, mem).start()
        for mem in (1, 5, 2, 4, 3):
            for half in range(2):
                share_copy(half, mem).start()

    adjoint = jnp.concatenate(
        [member_columns(member, half) * share[half] for member in range(2) for half in range(2)], axis=0
    )
    lift[...] = jnp.dot(upper_matrix[...], adjoint, precision=lax.Precision.HIGHEST,
                        preferred_element_type=F32)

    def block_copy(side, position, row):
        return remote(lift.at[tiles(WIDE * position, WIDE), :], relay.at[side],
                      block_sems.at[side, 0], block_sems.at[side, 1],
                      lev=WIDE * position + across, row=row)

    @pl.when(from_low == 1)
    def _():
        for position in (3, 2, 1, 0):
            block_copy(0, position, r - 1).start()

    @pl.when(from_high == 1)
    def _():
        for position in range(4):
            block_copy(1, position, r + 1).start()

    for apart in FAR_FIRST:
        for turn in range(4):
            if apart or turn:
                peer = WIDE * lax.rem(along + turn, 4) + lax.rem(across + apart, WIDE)
                remote(lift.at[tiles(peer, 1), :], back_fields.at[0, tiles(FIRST + l, 1), :],
                       back_sems.at[0], back_sems.at[1], lev=peer).start()

    back_fields[0, tiles(FIRST + l, 1), :] = lift[tiles(l, 1), :]

    def landing(side):
        return FIRST + LATS if side == 0 else 0

    def hand_on(side):
        block_copy(side, along, r).wait_recv()
        for apart in FAR_FIRST[:-1]:
            column = lax.rem(across + apart, WIDE)
            remote(relay.at[side, tiles(column, 1), :],
                   back_fields.at[0, tiles(landing(side) + across, 1), :],
                   relay_sems.at[side, 0], relay_sems.at[side, 1], lev=WIDE * along + column).start()
        back_fields[0, tiles(landing(side) + across, 1), :] = relay[side, tiles(across, 1), :]

    def handed(side):
        return remote(relay.at[side, tiles(0, WIDE - 1), :],
                      back_fields.at[0, tiles(landing(side), WIDE - 1), :],
                      relay_sems.at[side, 0], relay_sems.at[side, 1], lev=l)

    @pl.when(r > 0)
    def _():
        hand_on(1)

    @pl.when(r < BLOCKS - 1)
    def _():
        hand_on(0)

    columns = remote(lift.at[tiles(0, LEVS - 1), :], back_fields.at[0, tiles(FIRST, LEVS - 1), :],
                     back_sems.at[0], back_sems.at[1], lev=l)
    columns.wait_recv()
    diffuse_inside(back_fields, coefs)

    @pl.when(r > 0)
    def _():
        handed(1).wait_recv()

    @pl.when(r < BLOCKS - 1)
    def _():
        handed(0).wait_recv()

    diffuse_edges(back_fields, coefs, keep_lower)

    for member in range(2):
        for level in range(2):
            for half in range(2):
                lanes = slice(half * LANES, (half + 1) * LANES)
                smooth = back_fields[
                    PASSES, pl.ds(SUB * FIRST + sublane(member, level, half), LATS, stride=SUB), :
                ]
                out[member, level, :, lanes] = control[member, level, :, lanes].astype(F32) + smooth

    store = pltpu.make_async_copy(out, out_hbm, local_sems.at[0])
    store.start()

    @pl.when(r > 0)
    def _():
        for copy in edge_copies(0, r - 1):
            copy.wait_send()
        handed(1).wait_send()

    @pl.when(r < BLOCKS - 1)
    def _():
        for copy in edge_copies(1, r + 1):
            copy.wait_send()
        handed(0).wait_send()

    everyone.wait_send()

    @pl.when(is_root == 0)
    def _():
        for half in range(2):
            term_copy(half).wait_send()

    @pl.when(is_root == 1)
    def _():
        for half in range(2):
            term_batch_like = remote(parts.at[pl.ds(0, MEMS - 1), half], parts.at[pl.ds(0, MEMS - 1), half],
                                     share_sems.at[0, half], share_sems.at[1, half], mem=ROOT)
            term_batch_like.wait_send()

    def blocks_sent(side):
        return remote(lift.at[tiles(0, LEVS), :], lift.at[tiles(0, LEVS), :],
                      block_sems.at[side, 0], block_sems.at[side, 1], lev=l)

    @pl.when(from_low == 1)
    def _():
        blocks_sent(0).wait_send()

    @pl.when(from_high == 1)
    def _():
        blocks_sent(1).wait_send()

    columns.wait_send()
    store.wait()


def per_device(
    control, members, east_coef, south_coef, innovation, huber_class, band, level_group_index
):
    hbm = pl.BlockSpec(memory_space=pl.ANY)
    dma = pltpu.SemaphoreType.DMA
    group = level_group_index.reshape(1, -1)
    rows = pltpu.VMEM((SUB * ROWS, LANES), F32)
    return pl.pallas_call(
        kernel,
        out_shape=jax.ShapeDtypeStruct(control.shape, F32),
        in_specs=[hbm] * 8,
        out_specs=hbm,
        scratch_shapes=[
            pltpu.VMEM(control.shape, jnp.bfloat16),
            pltpu.VMEM(members.shape, jnp.bfloat16),
            pltpu.VMEM(east_coef.shape, F32),
            pltpu.VMEM(south_coef.shape, F32),
            pltpu.VMEM(innovation.shape, F32),
            pltpu.VMEM(huber_class.shape, jnp.int32),
            pltpu.VMEM(band.shape, F32),
            pltpu.VMEM(group.shape, jnp.int32),
            pltpu.VMEM(control.shape, F32),
            rows,
            rows,
            rows,
            pltpu.VMEM((PASSES + 1, SUB * ROWS, LANES), F32),
            pltpu.VMEM((PASSES + 1, SUB * ROWS, LANES), F32),
            pltpu.VMEM((2, 2, HALO, 2 * LANES), F32),
            pltpu.VMEM((2, 2, HALO, 2 * LANES), F32),
            pltpu.VMEM((SUB * LEVS, LANES), F32),
            pltpu.VMEM((SUB * LEVS, LANES), F32),
            pltpu.VMEM((2, SUB * WIDE, LANES), F32),
            pltpu.VMEM((256, 256), F32),
            pltpu.VMEM((256, 256), F32),
            pltpu.VMEM((2, 64, LANES), F32),
            pltpu.VMEM((MEMS - 1, 2, 64, LANES), F32),
            pltpu.VMEM((2, 64, LANES), F32),
            dma((8,)),
            dma((2, 3)),
            dma((2, 3)),
            dma((2,)),
            dma((2, 2)),
            dma((2, 2)),
            dma((2,)),
            dma((2, 2)),
            dma((2, 2)),
            pltpu.SemaphoreType.REGULAR,
            pltpu.SemaphoreType.REGULAR,
        ],
        compiler_params=pltpu.CompilerParams(collective_id=0, has_side_effects=True),
        name="hybrid_gradient",
    )(control, members, east_coef, south_coef, innovation, huber_class, band, group)


def solution(mesh):
    placed = (
        P("mem", "lev", "row", None),
        P("mem", None, ("row", "lev")),
        P("lev", "row", None),
        P("lev", "row", None),
        P(None, ("row", "lev")),
        P(None, ("row", "lev")),
        P(),
        P(),
    )
    return jax.shard_map(
        per_device,
        mesh=mesh,
        in_specs=placed,
        out_specs=P("mem", "lev", "row", None),
        check_vma=False,
    )
```

```python
import jax
import jax.numpy as jnp
from jax import lax
from jax.experimental import pallas as pl
from jax.experimental.pallas import tpu as pltpu
from jax.sharding import PartitionSpec as P

PASSES = 8
HUBER = 1.0
MESH = pl.DeviceIdType.MESH
F32 = jnp.float32

LANES = 128
SUB = 8
LATS = 32
HALO = 8
FIRST = HALO
ROWS = LATS + 2 * HALO
LEVS = 32
WIDE = 8
MEMS = 8
ROOT = MEMS - 1
BLOCKS = 4
FAR_FIRST = (4, 3, 5, 2, 6, 1, 7, 0)


def tiles(start, count):
    if isinstance(start, int):
        return pl.ds(SUB * start, SUB * count)
    return pl.ds(pl.multiple_of(SUB * start, SUB), SUB * count)


def sublane(member, level, half):
    return 4 * half + 2 * member + level


def next_longitude(x, lane):
    turned = pltpu.roll(x, LANES - 1, 2)
    return jnp.where(lane == LANES - 1, pltpu.roll(turned, 4, 1), turned)


def previous_longitude(x, lane):
    turned = pltpu.roll(x, 1, 2)
    return jnp.where(lane == 0, pltpu.roll(turned, 4, 1), turned)


def lane_index():
    return lax.broadcasted_iota(jnp.int32, (8, SUB, LANES), 2)


def one_pass(fields, coefs, step, start):
    east, west, south = coefs
    lane = lane_index()

    def field(row):
        return fields[step - 1, tiles(row, 8), :].reshape(8, SUB, LANES)

    def coef(ref, row):
        return ref[tiles(row, 8), :].reshape(8, SUB, LANES)

    center = field(start)
    flux_x = coef(east, start) * (next_longitude(center, lane) - center)
    flux_west = coef(west, start) * (center - previous_longitude(center, lane))
    flux_in = coef(south, start) * (center - field(start - 1))
    flux_out = coef(south, start + 1) * (field(start + 1) - center)
    return center + flux_x - flux_west + flux_out - flux_in


def diffuse_inside(fields, coefs):
    for step in range(1, PASSES + 1):
        starts = list(range(step, 24 - step, 8)) + [24 - step]
        for start in starts:
            result = one_pass(fields, coefs, step, FIRST + start)
            fields[step, tiles(FIRST + start, 8), :] = result.reshape(8 * SUB, LANES)


def diffuse_edges(fields, coefs, keep_lower):
    row = lax.broadcasted_iota(jnp.int32, (8, SUB, LANES), 0)

    @pl.loop(1, PASSES + 1)
    def _(step):
        low, high = FIRST - HALO + step, FIRST + LATS - step
        lower = one_pass(fields, coefs, step, low)
        upper = one_pass(fields, coefs, step, high)
        lower = lower * jnp.where(row + low >= FIRST, 1.0, keep_lower)
        fields[step, tiles(low, 8), :] = lower.reshape(8 * SUB, LANES)
        fields[step, tiles(high, 8), :] = upper.reshape(8 * SUB, LANES)


def vertical_columns(band_ref, group_ref, out_ref):
    band = band_ref[...]
    group = group_ref[...]
    group = jnp.concatenate([group, group], axis=1)
    coefs = []
    for offset in range(-3, 4):
        coef = band[offset + 3 : offset + 4, :] + (1.0 if offset == 0 else 0.0)
        coef = jnp.concatenate([coef, coef], axis=1)
        ahead = group if offset == 0 else pltpu.roll(group, (-offset) % LANES, 1)
        coef = jnp.where(ahead == group, coef, 0.0)
        coefs.append(jnp.concatenate([coef, coef], axis=1))

    @pl.loop(0, 8)
    def _(part):
        shape = (32, 256)
        row = lax.broadcasted_iota(jnp.int32, shape, 0) + 32 * part
        col = lax.broadcasted_iota(jnp.int32, shape, 1)
        half, member, level = (row // 4) % 2, (row // 2) % 2, row % 2
        apart = 2 * (row // SUB) + level + 1024 * (2 * member + half) - col % 64 - 1024 * (col // 64)
        total = jnp.zeros(shape, F32)
        for offset in range(-3, 4):
            total = jnp.where(apart == offset, coefs[offset + 3], total)
        out_ref[pl.ds(pl.multiple_of(32 * part, 32), 32), :] = total


def two_parts(x):
    high = x.astype(jnp.bfloat16)
    return high, (x - high.astype(F32)).astype(jnp.bfloat16)


def split_matrix(matrix, out_ref):
    high, low = two_parts(matrix)
    out_ref[:, 0:256] = high
    out_ref[:, 256:512] = high
    out_ref[:, 512:768] = low


def product(matrix_ref, x):
    high, low = two_parts(x)
    return jnp.dot(matrix_ref[...], jnp.concatenate([high, low, high], axis=0), preferred_element_type=F32)


def kernel(
    control_hbm, members_hbm, east_hbm, south_hbm, innovation_hbm, huber_hbm, band_hbm, group_hbm,
    out_hbm,
    control, members, east_in, south_in, innovation, huber, band, group, out,
    east, west, south, fields, back_fields, east_edge, south_edge,
    gathered, lift, relay, full_matrix, lower_matrix, upper_matrix,
    term, parts, share,
    local_sems, edge_send, edge_recv, fwd_sems, sum_sems, share_sems,
    back_sems, block_sems, relay_sems, lev_ready, mem_ready,
):
    m, l, r = lax.axis_index("mem"), lax.axis_index("lev"), lax.axis_index("row")
    along, across = l // WIDE, lax.rem(l, WIDE)
    has_lower = (r + BLOCKS - 1) // BLOCKS
    has_upper = 1 - (r + 1) // BLOCKS
    low_edge = 1 - (l + LEVS - HALO) // LEVS
    high_edge = (l + HALO) // LEVS
    from_low = low_edge * has_lower
    from_high = high_edge * has_upper
    coefs = (east, west, south)

    def leader(row):
        return 28 - 24 * (row // 2)

    is_leader = jnp.where(l == leader(r), 1, 0)
    is_root = m // ROOT

    def remote(source, target, send, recv, **where):
        return pltpu.make_async_remote_copy(
            src_ref=source, dst_ref=target, send_sem=send, recv_sem=recv,
            device_id=where, device_id_type=MESH,
        )

    barrier = pltpu.get_barrier_semaphore()

    def tell(sem, **where):
        pl.semaphore_signal(sem, inc=1, device_id=where, device_id_type=MESH)

    @pl.when(r > 0)
    def _():
        tell(barrier, row=r - 1)

    @pl.when(r < BLOCKS - 1)
    def _():
        tell(barrier, row=r + 1)

    @pl.when(is_leader == 0)
    def _():
        tell(barrier, lev=leader(r))

    @pl.when(is_root == 0)
    def _():
        tell(barrier, mem=ROOT)

    @pl.when(from_low == 1)
    def _():
        tell(barrier, lev=leader(r - 1), row=r - 1)

    @pl.when(from_high == 1)
    def _():
        tell(barrier, lev=leader(r + 1), row=r + 1)

    loads = [
        pltpu.make_async_copy(source, target, local_sems.at[i])
        for i, (source, target) in enumerate([
            (control_hbm, control), (east_hbm, east_in), (south_hbm, south_in),
            (band_hbm, band), (group_hbm, group),
            (members_hbm, members), (innovation_hbm, innovation), (huber_hbm, huber),
        ])
    ]
    for load in loads:
        load.start()

    blank = jnp.zeros((HALO * SUB, LANES), F32)
    halo_refs = (east, west, south, fields.at[0], back_fields.at[0])

    @pl.when(r == 0)
    def _():
        for ref in halo_refs:
            ref[tiles(0, HALO), :] = blank

    @pl.when(r == BLOCKS - 1)
    def _():
        for ref in halo_refs:
            ref[tiles(FIRST + LATS, HALO), :] = blank

    loads[0].wait()
    for member in range(2):
        for level in range(2):
            own = control[member, level].astype(F32)
            for half in range(2):
                fields[0, pl.ds(SUB * FIRST + sublane(member, level, half), LATS, stride=SUB), :] = own[
                    :, half * LANES : (half + 1) * LANES
                ]
    loads[1].wait()
    loads[2].wait()

    pl.semaphore_wait(
        barrier,
        has_lower + has_upper + is_root * (MEMS - 1)
        + is_leader * (LEVS - 1 + HALO * (has_lower + has_upper)),
    )

    def edge_copies(side, row):
        edge = slice(0, HALO) if side == 0 else slice(LATS - HALO, LATS)
        first = FIRST if side == 0 else FIRST + LATS - HALO
        landing = FIRST + LATS if side == 0 else 0
        return [
            remote(fields.at[0, tiles(first, HALO), :], fields.at[0, tiles(landing, HALO), :],
                   edge_send.at[side, 0], edge_recv.at[side, 0], row=row),
            remote(east_in.at[:, edge, :], east_edge.at[side],
                   edge_send.at[side, 1], edge_recv.at[side, 1], row=row),
            remote(south_in.at[:, edge, :], south_edge.at[side],
                   edge_send.at[side, 2], edge_recv.at[side, 2], row=row),
        ]

    @pl.when(r > 0)
    def _():
        for copy in edge_copies(0, r - 1):
            copy.start()

    @pl.when(r < BLOCKS - 1)
    def _():
        for copy in edge_copies(1, r + 1):
            copy.start()

    @pl.when(is_leader == 1)
    def _():
        @pl.loop(1, LEVS)
        def _(i):
            tell(lev_ready, lev=lax.rem(l + i, LEVS))

        @pl.when(r < BLOCKS - 1)
        def _():
            @pl.loop(0, HALO)
            def _(i):
                tell(lev_ready, lev=i, row=r + 1)

        @pl.when(r > 0)
        def _():
            @pl.loop(0, HALO)
            def _(i):
                tell(lev_ready, lev=LEVS - HALO + i, row=r - 1)

    @pl.when(is_root == 1)
    def _():
        @pl.loop(0, MEMS - 1)
        def _(i):
            tell(mem_ready, mem=i)

    def place(target, value, level, first, count):
        for half in range(2):
            for member in range(2):
                target[pl.ds(SUB * first + sublane(member, level, half), count, stride=SUB), :] = value[
                    :, half * LANES : (half + 1) * LANES
                ]

    def set_west(first):
        value = east[tiles(first, 8), :].reshape(8, SUB, LANES)
        west[tiles(first, 8), :] = previous_longitude(value, lane_index()).reshape(8 * SUB, LANES)

    for level in range(2):
        place(east, east_in[level], level, FIRST, LATS)
        place(south, south_in[level], level, FIRST, LATS)
    for first in range(FIRST, FIRST + LATS, 8):
        set_west(first)
    diffuse_inside(fields, coefs)

    pl.semaphore_wait(lev_ready, 1 - is_leader + from_low + from_high)

    def send_latitudes(rows):
        for apart in FAR_FIRST:
            for row in rows:
                peer = WIDE * row + lax.rem(across + apart, WIDE)

                def send(peer=peer):
                    remote(fields.at[PASSES, tiles(FIRST + peer, 1), :], gathered.at[tiles(l, 1), :],
                           fwd_sems.at[0], fwd_sems.at[1], lev=peer).start()

                if apart:
                    send()
                else:
                    pl.when(along != row)(send)

    send_latitudes((1, 2))

    for load in loads[3:]:
        load.wait()
    vertical_columns(band, group, full_matrix)
    split_matrix(full_matrix[...], upper_matrix)
    split_matrix(full_matrix[...].T, lower_matrix)

    def take_edge(side, first):
        for copy in edge_copies(side, r):
            copy.wait_recv()
        for level in range(2):
            place(east, east_edge[side, level], level, first, HALO)
            place(south, south_edge[side, level], level, first, HALO)
        set_west(first)

    @pl.when(r < BLOCKS - 1)
    def _():
        take_edge(0, FIRST + LATS)

    @pl.when(r > 0)
    def _():
        take_edge(1, 0)

    keep_lower = has_lower.astype(F32)
    diffuse_edges(fields, coefs, keep_lower)
    send_latitudes((0, 3))

    gathered[tiles(l, 1), :] = fields[PASSES, tiles(FIRST + l, 1), :]
    everyone = remote(fields.at[PASSES, tiles(FIRST, LEVS - 1), :], gathered.at[tiles(0, LEVS - 1), :],
                      fwd_sems.at[0], fwd_sems.at[1], lev=l)
    everyone.wait_recv()

    filtered = product(lower_matrix, gathered[...])

    def member_columns(member, half):
        return members[member, :, half * LANES : (half + 1) * LANES].astype(F32)

    for half in range(2):
        term[half] = sum(
            member_columns(member, half) * filtered[64 * (2 * member + half) : 64 * (2 * member + half + 1)]
            for member in range(2)
        )

    roots = (ROOT, 0)
    orders = ((0, 6, 1, 5, 2, 4, 3), (1, 7, 2, 6, 3, 5, 4))

    def term_copy(half):
        return remote(term.at[half], parts.at[m - half, half], sum_sems.at[0, half], sum_sems.at[1, half],
                      mem=roots[half])

    def share_copy(half, mem):
        return remote(share.at[half], share.at[half], share_sems.at[0, half], share_sems.at[1, half], mem=mem)

    def rest(half, sems):
        others = parts.at[pl.ds(0, MEMS - 1), half]
        return remote(others, others, sems.at[0, half], sems.at[1, half], mem=m)

    def gather_half(half):
        rest(half, sum_sems).wait_recv()
        values = [parts[i, half] for i in range(MEMS - 1)]
        values.insert(roots[half], term[half])
        increment = values[0]
        for value in values[1:]:
            increment = increment + value
        lanes = slice(half * LANES, (half + 1) * LANES)
        residual = increment - innovation[:, lanes]
        scale = HUBER / jnp.maximum(jnp.abs(residual), HUBER)
        share[half] = jnp.where(huber[:, lanes] == 1, scale, 1.0) * residual
        for mem in orders[half]:
            share_copy(half, mem).start()

    @pl.when(is_root == 0)
    def _():
        pl.semaphore_wait(mem_ready, 1)
        term_copy(0).start()

    @pl.when(m > 0)
    def _():
        term_copy(1).start()

    @pl.when(is_root == 1)
    def _():
        gather_half(0)
        share_copy(1, 0).wait_recv()

    @pl.when(m == 0)
    def _():
        gather_half(1)
        share_copy(0, 0).wait_recv()

    @pl.when((m > 0) & (is_root == 0))
    def _():
        for half in range(2):
            share_copy(half, 0).wait_recv()

    adjoint = jnp.concatenate(
        [member_columns(member, half) * share[half] for member in range(2) for half in range(2)], axis=0
    )
    lift[...] = product(upper_matrix, adjoint)

    def block_copy(side, position, row):
        return remote(lift.at[tiles(WIDE * position, WIDE), :], relay.at[side],
                      block_sems.at[side, 0], block_sems.at[side, 1],
                      lev=WIDE * position + across, row=row)

    def landing(side):
        return FIRST + LATS if side == 0 else 0

    def direct_copy(side, column, row):
        return remote(lift.at[tiles(column, 1), :], back_fields.at[0, tiles(landing(side) + across, 1), :],
                      block_sems.at[side, 2], relay_sems.at[side, 1], lev=column, row=row)

    def send_edges(side, positions, row):
        for apart in FAR_FIRST:
            direct_copy(side, lax.rem(across + apart, WIDE), row).start()
        for position in positions:
            block_copy(side, position, row).start()

    @pl.when(from_low == 1)
    def _():
        send_edges(0, (1, 2, 3), r - 1)

    @pl.when(from_high == 1)
    def _():
        send_edges(1, (3, 2, 1), r + 1)

    for apart in FAR_FIRST:
        for turn in range(4):
            if apart or turn:
                peer = WIDE * lax.rem(along + turn, 4) + lax.rem(across + apart, WIDE)
                remote(lift.at[tiles(peer, 1), :], back_fields.at[0, tiles(FIRST + l, 1), :],
                       back_sems.at[0], back_sems.at[1], lev=peer).start()

    back_fields[0, tiles(FIRST + l, 1), :] = lift[tiles(l, 1), :]

    def hand_on(side):
        block_copy(side, along, r).wait_recv()
        for apart in FAR_FIRST[:-1]:
            column = lax.rem(across + apart, WIDE)
            remote(relay.at[side, tiles(column, 1), :],
                   back_fields.at[0, tiles(landing(side) + across, 1), :],
                   relay_sems.at[side, 0], relay_sems.at[side, 1], lev=WIDE * along + column).start()
        back_fields[0, tiles(landing(side) + across, 1), :] = relay[side, tiles(across, 1), :]

    def handed(side, count):
        return remote(relay.at[side, tiles(0, count), :],
                      back_fields.at[0, tiles(landing(side), count), :],
                      relay_sems.at[side, 0], relay_sems.at[side, 1], lev=l)

    @pl.when((r > 0) & (along > 0))
    def _():
        hand_on(1)

    @pl.when((r < BLOCKS - 1) & (along > 0))
    def _():
        hand_on(0)

    columns = remote(lift.at[tiles(0, LEVS - 1), :], back_fields.at[0, tiles(FIRST, LEVS - 1), :],
                     back_sems.at[0], back_sems.at[1], lev=l)
    columns.wait_recv()
    diffuse_inside(back_fields, coefs)

    def halo_arrived(side):
        @pl.when(along > 0)
        def _():
            handed(side, WIDE - 1).wait_recv()

        @pl.when(along == 0)
        def _():
            handed(side, WIDE).wait_recv()

    @pl.when(r > 0)
    def _():
        halo_arrived(1)

    @pl.when(r < BLOCKS - 1)
    def _():
        halo_arrived(0)

    diffuse_edges(back_fields, coefs, keep_lower)

    for member in range(2):
        for level in range(2):
            for half in range(2):
                lanes = slice(half * LANES, (half + 1) * LANES)
                smooth = back_fields[
                    PASSES, pl.ds(SUB * FIRST + sublane(member, level, half), LATS, stride=SUB), :
                ]
                out[member, level, :, lanes] = control[member, level, :, lanes].astype(F32) + smooth

    store = pltpu.make_async_copy(out, out_hbm, local_sems.at[0])
    store.start()

    @pl.when(r > 0)
    def _():
        for copy in edge_copies(0, r - 1):
            copy.wait_send()

        @pl.when(along > 0)
        def _():
            handed(1, WIDE - 1).wait_send()

    @pl.when(r < BLOCKS - 1)
    def _():
        for copy in edge_copies(1, r + 1):
            copy.wait_send()

        @pl.when(along > 0)
        def _():
            handed(0, WIDE - 1).wait_send()

    everyone.wait_send()

    @pl.when(is_root == 0)
    def _():
        term_copy(0).wait_send()

    @pl.when(m > 0)
    def _():
        term_copy(1).wait_send()

    @pl.when(is_root == 1)
    def _():
        rest(0, share_sems).wait_send()

    @pl.when(m == 0)
    def _():
        rest(1, share_sems).wait_send()

    def edges_sent(side):
        for way, count in ((0, LEVS - WIDE), (2, WIDE)):
            remote(lift.at[tiles(0, count), :], lift.at[tiles(0, count), :],
                   block_sems.at[side, way], block_sems.at[side, 1], lev=l).wait_send()

    @pl.when(from_low == 1)
    def _():
        edges_sent(0)

    @pl.when(from_high == 1)
    def _():
        edges_sent(1)

    columns.wait_send()
    store.wait()


def per_device(
    control, members, east_coef, south_coef, innovation, huber_class, band, level_group_index
):
    hbm = pl.BlockSpec(memory_space=pl.ANY)
    dma = pltpu.SemaphoreType.DMA
    group = level_group_index.reshape(1, -1)
    rows = pltpu.VMEM((SUB * ROWS, LANES), F32)
    return pl.pallas_call(
        kernel,
        out_shape=jax.ShapeDtypeStruct(control.shape, F32),
        in_specs=[hbm] * 8,
        out_specs=hbm,
        scratch_shapes=[
            pltpu.VMEM(control.shape, jnp.bfloat16),
            pltpu.VMEM(members.shape, jnp.bfloat16),
            pltpu.VMEM(east_coef.shape, F32),
            pltpu.VMEM(south_coef.shape, F32),
            pltpu.VMEM(innovation.shape, F32),
            pltpu.VMEM(huber_class.shape, jnp.int32),
            pltpu.VMEM(band.shape, F32),
            pltpu.VMEM(group.shape, jnp.int32),
            pltpu.VMEM(control.shape, F32),
            rows,
            rows,
            rows,
            pltpu.VMEM((PASSES + 1, SUB * ROWS, LANES), F32),
            pltpu.VMEM((PASSES + 1, SUB * ROWS, LANES), F32),
            pltpu.VMEM((2, 2, HALO, 2 * LANES), F32),
            pltpu.VMEM((2, 2, HALO, 2 * LANES), F32),
            pltpu.VMEM((SUB * LEVS, LANES), F32),
            pltpu.VMEM((SUB * LEVS, LANES), F32),
            pltpu.VMEM((2, SUB * WIDE, LANES), F32),
            pltpu.VMEM((256, 256), F32),
            pltpu.VMEM((256, 768), jnp.bfloat16),
            pltpu.VMEM((256, 768), jnp.bfloat16),
            pltpu.VMEM((2, 64, LANES), F32),
            pltpu.VMEM((MEMS - 1, 2, 64, LANES), F32),
            pltpu.VMEM((2, 64, LANES), F32),
            dma((8,)),
            dma((2, 3)),
            dma((2, 3)),
            dma((2,)),
            dma((2, 2)),
            dma((2, 2)),
            dma((2,)),
            dma((2, 3)),
            dma((2, 2)),
            pltpu.SemaphoreType.REGULAR,
            pltpu.SemaphoreType.REGULAR,
        ],
        compiler_params=pltpu.CompilerParams(collective_id=0, has_side_effects=True),
        name="hybrid_gradient",
    )(control, members, east_coef, south_coef, innovation, huber_class, band, group)


def solution(mesh):
    placed = (
        P("mem", "lev", "row", None),
        P("mem", None, ("row", "lev")),
        P("lev", "row", None),
        P("lev", "row", None),
        P(None, ("row", "lev")),
        P(None, ("row", "lev")),
        P(),
        P(),
    )
    return jax.shard_map(
        per_device,
        mesh=mesh,
        in_specs=placed,
        out_specs=P("mem", "lev", "row", None),
        check_vma=False,
    )
```

```python
import jax
import jax.numpy as jnp
from jax import lax
from jax.experimental import pallas as pl
from jax.experimental.pallas import tpu as pltpu
from jax.sharding import PartitionSpec as P

PASSES = 8
HUBER = 1.0
MESH = pl.DeviceIdType.MESH
F32 = jnp.float32

LANES = 128
SUB = 8
LATS = 32
HALO = 8
FIRST = HALO
ROWS = LATS + 2 * HALO
LEVS = 32
WIDE = 8
MEMS = 8
ROOT = MEMS - 1
DIRECT = 2
BLOCKS = 4
FAR_FIRST = (4, 3, 5, 2, 6, 1, 7, 0)


def tiles(start, count):
    if isinstance(start, int):
        return pl.ds(SUB * start, SUB * count)
    return pl.ds(pl.multiple_of(SUB * start, SUB), SUB * count)


def sublane(member, level, half):
    return 4 * half + 2 * member + level


def next_longitude(x, lane):
    turned = pltpu.roll(x, LANES - 1, 2)
    return jnp.where(lane == LANES - 1, pltpu.roll(turned, 4, 1), turned)


def previous_longitude(x, lane):
    turned = pltpu.roll(x, 1, 2)
    return jnp.where(lane == 0, pltpu.roll(turned, 4, 1), turned)


def lane_index():
    return lax.broadcasted_iota(jnp.int32, (8, SUB, LANES), 2)


def one_pass(fields, coefs, step, start):
    east, west, south = coefs
    lane = lane_index()

    def field(row):
        return fields[step - 1, tiles(row, 8), :].reshape(8, SUB, LANES)

    def coef(ref, row):
        return ref[tiles(row, 8), :].reshape(8, SUB, LANES)

    center = field(start)
    flux_x = coef(east, start) * (next_longitude(center, lane) - center)
    flux_west = coef(west, start) * (center - previous_longitude(center, lane))
    flux_in = coef(south, start) * (center - field(start - 1))
    flux_out = coef(south, start + 1) * (field(start + 1) - center)
    return center + flux_x - flux_west + flux_out - flux_in


def diffuse_inside(fields, coefs):
    for step in range(1, PASSES + 1):
        starts = list(range(step, 24 - step, 8)) + [24 - step]
        for start in starts:
            result = one_pass(fields, coefs, step, FIRST + start)
            fields[step, tiles(FIRST + start, 8), :] = result.reshape(8 * SUB, LANES)


def diffuse_edges(fields, coefs, keep_lower):
    row = lax.broadcasted_iota(jnp.int32, (8, SUB, LANES), 0)

    @pl.loop(1, PASSES + 1)
    def _(step):
        low, high = FIRST - HALO + step, FIRST + LATS - step
        lower = one_pass(fields, coefs, step, low)
        upper = one_pass(fields, coefs, step, high)
        lower = lower * jnp.where(row + low >= FIRST, 1.0, keep_lower)
        fields[step, tiles(low, 8), :] = lower.reshape(8 * SUB, LANES)
        fields[step, tiles(high, 8), :] = upper.reshape(8 * SUB, LANES)


def vertical_columns(band_ref, group_ref, out_ref):
    band = band_ref[...]
    group = group_ref[...]
    group = jnp.concatenate([group, group], axis=1)
    coefs = []
    for offset in range(-3, 4):
        coef = band[offset + 3 : offset + 4, :] + (1.0 if offset == 0 else 0.0)
        coef = jnp.concatenate([coef, coef], axis=1)
        ahead = group if offset == 0 else pltpu.roll(group, (-offset) % LANES, 1)
        coef = jnp.where(ahead == group, coef, 0.0)
        coefs.append(jnp.concatenate([coef, coef], axis=1))

    @pl.loop(0, 8)
    def _(part):
        shape = (32, 256)
        row = lax.broadcasted_iota(jnp.int32, shape, 0) + 32 * part
        col = lax.broadcasted_iota(jnp.int32, shape, 1)
        half, member, level = (row // 4) % 2, (row // 2) % 2, row % 2
        apart = 2 * (row // SUB) + level + 1024 * (2 * member + half) - col % 64 - 1024 * (col // 64)
        total = jnp.zeros(shape, F32)
        for offset in range(-3, 4):
            total = jnp.where(apart == offset, coefs[offset + 3], total)
        out_ref[pl.ds(pl.multiple_of(32 * part, 32), 32), :] = total


def two_parts(x):
    high = x.astype(jnp.bfloat16)
    return high, (x - high.astype(F32)).astype(jnp.bfloat16)


def split_matrix(matrix, out_ref):
    high, low = two_parts(matrix)
    out_ref[:, 0:256] = high
    out_ref[:, 256:512] = high
    out_ref[:, 512:768] = low


def product(matrix_ref, x):
    high, low = two_parts(x)
    return jnp.dot(matrix_ref[...], jnp.concatenate([high, low, high], axis=0), preferred_element_type=F32)


def kernel(
    control_hbm, members_hbm, east_hbm, south_hbm, innovation_hbm, huber_hbm, band_hbm, group_hbm,
    out_hbm,
    control, members, east_in, south_in, innovation, huber, band, group, out,
    east, west, south, fields, back_fields, east_edge, south_edge,
    gathered, lift, relay, full_matrix, lower_matrix, upper_matrix,
    term, parts, share,
    local_sems, edge_send, edge_recv, fwd_sems, sum_sems, share_sems,
    back_sems, block_sems, relay_sems, lev_ready, mem_ready,
):
    m, l, r = lax.axis_index("mem"), lax.axis_index("lev"), lax.axis_index("row")
    along, across = l // WIDE, lax.rem(l, WIDE)
    has_lower = (r + BLOCKS - 1) // BLOCKS
    has_upper = 1 - (r + 1) // BLOCKS
    low_edge = 1 - (l + LEVS - HALO) // LEVS
    high_edge = (l + HALO) // LEVS
    from_low = low_edge * has_lower
    from_high = high_edge * has_upper
    coefs = (east, west, south)

    def leader(row):
        return 28 - 24 * (row // 2)

    is_leader = jnp.where(l == leader(r), 1, 0)
    is_root = m // ROOT

    def remote(source, target, send, recv, **where):
        return pltpu.make_async_remote_copy(
            src_ref=source, dst_ref=target, send_sem=send, recv_sem=recv,
            device_id=where, device_id_type=MESH,
        )

    barrier = pltpu.get_barrier_semaphore()

    def tell(sem, **where):
        pl.semaphore_signal(sem, inc=1, device_id=where, device_id_type=MESH)

    @pl.when(r > 0)
    def _():
        tell(barrier, row=r - 1)

    @pl.when(r < BLOCKS - 1)
    def _():
        tell(barrier, row=r + 1)

    @pl.when(is_leader == 0)
    def _():
        tell(barrier, lev=leader(r))

    @pl.when(is_root == 0)
    def _():
        tell(barrier, mem=ROOT)

    @pl.when(from_low == 1)
    def _():
        tell(barrier, lev=leader(r - 1), row=r - 1)

    @pl.when(from_high == 1)
    def _():
        tell(barrier, lev=leader(r + 1), row=r + 1)

    loads = [
        pltpu.make_async_copy(source, target, local_sems.at[i])
        for i, (source, target) in enumerate([
            (control_hbm, control), (east_hbm, east_in), (south_hbm, south_in),
            (band_hbm, band), (group_hbm, group),
            (members_hbm, members), (innovation_hbm, innovation), (huber_hbm, huber),
        ])
    ]
    for load in loads:
        load.start()

    blank = jnp.zeros((HALO * SUB, LANES), F32)
    halo_refs = (east, west, south, fields.at[0], back_fields.at[0])

    @pl.when(r == 0)
    def _():
        for ref in halo_refs:
            ref[tiles(0, HALO), :] = blank

    @pl.when(r == BLOCKS - 1)
    def _():
        for ref in halo_refs:
            ref[tiles(FIRST + LATS, HALO), :] = blank

    loads[0].wait()
    for member in range(2):
        for level in range(2):
            own = control[member, level].astype(F32)
            for half in range(2):
                fields[0, pl.ds(SUB * FIRST + sublane(member, level, half), LATS, stride=SUB), :] = own[
                    :, half * LANES : (half + 1) * LANES
                ]
    loads[1].wait()
    loads[2].wait()

    pl.semaphore_wait(
        barrier,
        has_lower + has_upper + is_root * (MEMS - 1)
        + is_leader * (LEVS - 1 + HALO * (has_lower + has_upper)),
    )

    def edge_copies(side, row):
        edge = slice(0, HALO) if side == 0 else slice(LATS - HALO, LATS)
        first = FIRST if side == 0 else FIRST + LATS - HALO
        landing = FIRST + LATS if side == 0 else 0
        return [
            remote(fields.at[0, tiles(first, HALO), :], fields.at[0, tiles(landing, HALO), :],
                   edge_send.at[side, 0], edge_recv.at[side, 0], row=row),
            remote(east_in.at[:, edge, :], east_edge.at[side],
                   edge_send.at[side, 1], edge_recv.at[side, 1], row=row),
            remote(south_in.at[:, edge, :], south_edge.at[side],
                   edge_send.at[side, 2], edge_recv.at[side, 2], row=row),
        ]

    @pl.when(r > 0)
    def _():
        for copy in edge_copies(0, r - 1):
            copy.start()

    @pl.when(r < BLOCKS - 1)
    def _():
        for copy in edge_copies(1, r + 1):
            copy.start()

    @pl.when(is_leader == 1)
    def _():
        @pl.loop(1, LEVS)
        def _(i):
            tell(lev_ready, lev=lax.rem(l + i, LEVS))

        @pl.when(r < BLOCKS - 1)
        def _():
            @pl.loop(0, HALO)
            def _(i):
                tell(lev_ready, lev=i, row=r + 1)

        @pl.when(r > 0)
        def _():
            @pl.loop(0, HALO)
            def _(i):
                tell(lev_ready, lev=LEVS - HALO + i, row=r - 1)

    @pl.when(is_root == 1)
    def _():
        @pl.loop(0, MEMS - 1)
        def _(i):
            tell(mem_ready, mem=i)

    def place(target, value, level, first, count):
        for half in range(2):
            for member in range(2):
                target[pl.ds(SUB * first + sublane(member, level, half), count, stride=SUB), :] = value[
                    :, half * LANES : (half + 1) * LANES
                ]

    def set_west(first):
        value = east[tiles(first, 8), :].reshape(8, SUB, LANES)
        west[tiles(first, 8), :] = previous_longitude(value, lane_index()).reshape(8 * SUB, LANES)

    for level in range(2):
        place(east, east_in[level], level, FIRST, LATS)
        place(south, south_in[level], level, FIRST, LATS)
    for first in range(FIRST, FIRST + LATS, 8):
        set_west(first)
    diffuse_inside(fields, coefs)

    pl.semaphore_wait(lev_ready, 1 - is_leader + from_low + from_high)

    def send_latitudes(rows):
        for apart in FAR_FIRST:
            for row in rows:
                peer = WIDE * row + lax.rem(across + apart, WIDE)

                def send(peer=peer):
                    remote(fields.at[PASSES, tiles(FIRST + peer, 1), :], gathered.at[tiles(l, 1), :],
                           fwd_sems.at[0], fwd_sems.at[1], lev=peer).start()

                if apart:
                    send()
                else:
                    pl.when(along != row)(send)

    send_latitudes((1, 2))

    for load in loads[3:]:
        load.wait()
    vertical_columns(band, group, full_matrix)
    split_matrix(full_matrix[...], upper_matrix)
    split_matrix(full_matrix[...].T, lower_matrix)

    def take_edge(side, first):
        for copy in edge_copies(side, r):
            copy.wait_recv()
        for level in range(2):
            place(east, east_edge[side, level], level, first, HALO)
            place(south, south_edge[side, level], level, first, HALO)
        set_west(first)

    @pl.when(r < BLOCKS - 1)
    def _():
        take_edge(0, FIRST + LATS)

    @pl.when(r > 0)
    def _():
        take_edge(1, 0)

    keep_lower = has_lower.astype(F32)
    diffuse_edges(fields, coefs, keep_lower)
    send_latitudes((0, 3))

    gathered[tiles(l, 1), :] = fields[PASSES, tiles(FIRST + l, 1), :]
    everyone = remote(fields.at[PASSES, tiles(FIRST, LEVS - 1), :], gathered.at[tiles(0, LEVS - 1), :],
                      fwd_sems.at[0], fwd_sems.at[1], lev=l)
    everyone.wait_recv()

    filtered = product(lower_matrix, gathered[...])

    def member_columns(member, half):
        return members[member, :, half * LANES : (half + 1) * LANES].astype(F32)

    for half in range(2):
        term[half] = sum(
            member_columns(member, half) * filtered[64 * (2 * member + half) : 64 * (2 * member + half + 1)]
            for member in range(2)
        )

    roots = (ROOT, 0)
    orders = ((0, 6, 1, 5, 2, 4, 3), (1, 7, 2, 6, 3, 5, 4))

    def term_copy(half):
        return remote(term.at[half], parts.at[m - half, half], sum_sems.at[0, half], sum_sems.at[1, half],
                      mem=roots[half])

    def share_copy(half, mem):
        return remote(share.at[half], share.at[half], share_sems.at[0, half], share_sems.at[1, half], mem=mem)

    def rest(half, sems):
        others = parts.at[pl.ds(0, MEMS - 1), half]
        return remote(others, others, sems.at[0, half], sems.at[1, half], mem=m)

    def gather_half(half):
        rest(half, sum_sems).wait_recv()
        values = [parts[i, half] for i in range(MEMS - 1)]
        values.insert(roots[half], term[half])
        increment = values[0]
        for value in values[1:]:
            increment = increment + value
        lanes = slice(half * LANES, (half + 1) * LANES)
        residual = increment - innovation[:, lanes]
        scale = HUBER / jnp.maximum(jnp.abs(residual), HUBER)
        share[half] = jnp.where(huber[:, lanes] == 1, scale, 1.0) * residual
        for mem in orders[half]:
            share_copy(half, mem).start()

    @pl.when(is_root == 0)
    def _():
        pl.semaphore_wait(mem_ready, 1)
        term_copy(0).start()

    @pl.when(m > 0)
    def _():
        term_copy(1).start()

    @pl.when(is_root == 1)
    def _():
        gather_half(0)
        share_copy(1, 0).wait_recv()

    @pl.when(m == 0)
    def _():
        gather_half(1)
        share_copy(0, 0).wait_recv()

    @pl.when((m > 0) & (is_root == 0))
    def _():
        for half in range(2):
            share_copy(half, 0).wait_recv()

    adjoint = jnp.concatenate(
        [member_columns(member, half) * share[half] for member in range(2) for half in range(2)], axis=0
    )
    lift[...] = product(upper_matrix, adjoint)

    def block_copy(side, position, row):
        return remote(lift.at[tiles(WIDE * position, WIDE), :], relay.at[side],
                      block_sems.at[side, 0], block_sems.at[side, 1],
                      lev=WIDE * position + across, row=row)

    def landing(side):
        return FIRST + LATS if side == 0 else 0

    def direct_copy(side, peer, row):
        return remote(lift.at[tiles(peer, 1), :], back_fields.at[0, tiles(landing(side) + across, 1), :],
                      block_sems.at[side, 2], relay_sems.at[side, 1], lev=peer, row=row)

    def send_edges(side, positions, row):
        for apart in FAR_FIRST:
            for position in range(DIRECT):
                direct_copy(side, WIDE * position + lax.rem(across + apart, WIDE), row).start()
        for position in positions:
            block_copy(side, position, row).start()

    @pl.when(from_low == 1)
    def _():
        send_edges(0, range(DIRECT, 4), r - 1)

    @pl.when(from_high == 1)
    def _():
        send_edges(1, range(3, DIRECT - 1, -1), r + 1)

    for apart in FAR_FIRST:
        for turn in range(4):
            if apart or turn:
                peer = WIDE * lax.rem(along + turn, 4) + lax.rem(across + apart, WIDE)
                remote(lift.at[tiles(peer, 1), :], back_fields.at[0, tiles(FIRST + l, 1), :],
                       back_sems.at[0], back_sems.at[1], lev=peer).start()

    back_fields[0, tiles(FIRST + l, 1), :] = lift[tiles(l, 1), :]

    def hand_on(side):
        block_copy(side, along, r).wait_recv()
        for apart in FAR_FIRST[:-1]:
            column = lax.rem(across + apart, WIDE)
            remote(relay.at[side, tiles(column, 1), :],
                   back_fields.at[0, tiles(landing(side) + across, 1), :],
                   relay_sems.at[side, 0], relay_sems.at[side, 1], lev=WIDE * along + column).start()
        back_fields[0, tiles(landing(side) + across, 1), :] = relay[side, tiles(across, 1), :]

    def handed(side, count):
        return remote(relay.at[side, tiles(0, count), :],
                      back_fields.at[0, tiles(landing(side), count), :],
                      relay_sems.at[side, 0], relay_sems.at[side, 1], lev=l)

    @pl.when((r > 0) & (along >= DIRECT))
    def _():
        hand_on(1)

    @pl.when((r < BLOCKS - 1) & (along >= DIRECT))
    def _():
        hand_on(0)

    columns = remote(lift.at[tiles(0, LEVS - 1), :], back_fields.at[0, tiles(FIRST, LEVS - 1), :],
                     back_sems.at[0], back_sems.at[1], lev=l)
    columns.wait_recv()
    diffuse_inside(back_fields, coefs)

    def halo_arrived(side):
        @pl.when(along >= DIRECT)
        def _():
            handed(side, WIDE - 1).wait_recv()

        @pl.when(along < DIRECT)
        def _():
            handed(side, WIDE).wait_recv()

    @pl.when(r > 0)
    def _():
        halo_arrived(1)

    @pl.when(r < BLOCKS - 1)
    def _():
        halo_arrived(0)

    diffuse_edges(back_fields, coefs, keep_lower)

    for member in range(2):
        for level in range(2):
            for half in range(2):
                lanes = slice(half * LANES, (half + 1) * LANES)
                smooth = back_fields[
                    PASSES, pl.ds(SUB * FIRST + sublane(member, level, half), LATS, stride=SUB), :
                ]
                out[member, level, :, lanes] = control[member, level, :, lanes].astype(F32) + smooth

    store = pltpu.make_async_copy(out, out_hbm, local_sems.at[0])
    store.start()

    @pl.when(r > 0)
    def _():
        for copy in edge_copies(0, r - 1):
            copy.wait_send()

        @pl.when(along >= DIRECT)
        def _():
            handed(1, WIDE - 1).wait_send()

    @pl.when(r < BLOCKS - 1)
    def _():
        for copy in edge_copies(1, r + 1):
            copy.wait_send()

        @pl.when(along >= DIRECT)
        def _():
            handed(0, WIDE - 1).wait_send()

    everyone.wait_send()

    @pl.when(is_root == 0)
    def _():
        term_copy(0).wait_send()

    @pl.when(m > 0)
    def _():
        term_copy(1).wait_send()

    @pl.when(is_root == 1)
    def _():
        rest(0, share_sems).wait_send()

    @pl.when(m == 0)
    def _():
        rest(1, share_sems).wait_send()

    def edges_sent(side):
        for way, count in ((0, LEVS - DIRECT * WIDE), (2, DIRECT * WIDE)):
            remote(lift.at[tiles(0, count), :], lift.at[tiles(0, count), :],
                   block_sems.at[side, way], block_sems.at[side, 1], lev=l).wait_send()

    @pl.when(from_low == 1)
    def _():
        edges_sent(0)

    @pl.when(from_high == 1)
    def _():
        edges_sent(1)

    columns.wait_send()
    store.wait()


def per_device(
    control, members, east_coef, south_coef, innovation, huber_class, band, level_group_index
):
    hbm = pl.BlockSpec(memory_space=pl.ANY)
    dma = pltpu.SemaphoreType.DMA
    group = level_group_index.reshape(1, -1)
    rows = pltpu.VMEM((SUB * ROWS, LANES), F32)
    return pl.pallas_call(
        kernel,
        out_shape=jax.ShapeDtypeStruct(control.shape, F32),
        in_specs=[hbm] * 8,
        out_specs=hbm,
        scratch_shapes=[
            pltpu.VMEM(control.shape, jnp.bfloat16),
            pltpu.VMEM(members.shape, jnp.bfloat16),
            pltpu.VMEM(east_coef.shape, F32),
            pltpu.VMEM(south_coef.shape, F32),
            pltpu.VMEM(innovation.shape, F32),
            pltpu.VMEM(huber_class.shape, jnp.int32),
            pltpu.VMEM(band.shape, F32),
            pltpu.VMEM(group.shape, jnp.int32),
            pltpu.VMEM(control.shape, F32),
            rows,
            rows,
            rows,
            pltpu.VMEM((PASSES + 1, SUB * ROWS, LANES), F32),
            pltpu.VMEM((PASSES + 1, SUB * ROWS, LANES), F32),
            pltpu.VMEM((2, 2, HALO, 2 * LANES), F32),
            pltpu.VMEM((2, 2, HALO, 2 * LANES), F32),
            pltpu.VMEM((SUB * LEVS, LANES), F32),
            pltpu.VMEM((SUB * LEVS, LANES), F32),
            pltpu.VMEM((2, SUB * WIDE, LANES), F32),
            pltpu.VMEM((256, 256), F32),
            pltpu.VMEM((256, 768), jnp.bfloat16),
            pltpu.VMEM((256, 768), jnp.bfloat16),
            pltpu.VMEM((2, 64, LANES), F32),
            pltpu.VMEM((MEMS - 1, 2, 64, LANES), F32),
            pltpu.VMEM((2, 64, LANES), F32),
            dma((8,)),
            dma((2, 3)),
            dma((2, 3)),
            dma((2,)),
            dma((2, 2)),
            dma((2, 2)),
            dma((2,)),
            dma((2, 3)),
            dma((2, 2)),
            pltpu.SemaphoreType.REGULAR,
            pltpu.SemaphoreType.REGULAR,
        ],
        compiler_params=pltpu.CompilerParams(collective_id=0, has_side_effects=True),
        name="hybrid_gradient",
    )(control, members, east_coef, south_coef, innovation, huber_class, band, group)


def solution(mesh):
    placed = (
        P("mem", "lev", "row", None),
        P("mem", None, ("row", "lev")),
        P("lev", "row", None),
        P("lev", "row", None),
        P(None, ("row", "lev")),
        P(None, ("row", "lev")),
        P(),
        P(),
    )
    return jax.shard_map(
        per_device,
        mesh=mesh,
        in_specs=placed,
        out_specs=P("mem", "lev", "row", None),
        check_vma=False,
    )
```

```python
import jax
import jax.numpy as jnp
from jax import lax
from jax.experimental import pallas as pl
from jax.experimental.pallas import tpu as pltpu
from jax.sharding import PartitionSpec as P

PASSES = 8
HUBER = 1.0
MESH = pl.DeviceIdType.MESH
F32 = jnp.float32

LANES = 128
SUB = 8
LATS = 32
HALO = 8
FIRST = HALO
ROWS = LATS + 2 * HALO
LEVS = 32
WIDE = 8
MEMS = 8
ROOT = MEMS - 1
DIRECT = 2
BLOCKS = 4
FAR_FIRST = (4, 3, 5, 2, 6, 1, 7, 0)


def tiles(start, count):
    if isinstance(start, int):
        return pl.ds(SUB * start, SUB * count)
    return pl.ds(pl.multiple_of(SUB * start, SUB), SUB * count)


def sublane(member, level, half):
    return 4 * half + 2 * member + level


def next_longitude(x, lane):
    turned = pltpu.roll(x, LANES - 1, 2)
    return jnp.where(lane == LANES - 1, pltpu.roll(turned, 4, 1), turned)


def previous_longitude(x, lane):
    turned = pltpu.roll(x, 1, 2)
    return jnp.where(lane == 0, pltpu.roll(turned, 4, 1), turned)


def lane_index():
    return lax.broadcasted_iota(jnp.int32, (8, SUB, LANES), 2)


def one_pass(fields, coefs, step, start):
    east, west, south = coefs
    lane = lane_index()

    def field(row):
        return fields[step - 1, tiles(row, 8), :].reshape(8, SUB, LANES)

    def coef(ref, row):
        return ref[tiles(row, 8), :].reshape(8, SUB, LANES)

    center = field(start)
    flux_x = coef(east, start) * (next_longitude(center, lane) - center)
    flux_west = coef(west, start) * (center - previous_longitude(center, lane))
    flux_in = coef(south, start) * (center - field(start - 1))
    flux_out = coef(south, start + 1) * (field(start + 1) - center)
    return center + flux_x - flux_west + flux_out - flux_in


def diffuse_inside(fields, coefs):
    for step in range(1, PASSES + 1):
        starts = list(range(step, 24 - step, 8)) + [24 - step]
        for start in starts:
            result = one_pass(fields, coefs, step, FIRST + start)
            fields[step, tiles(FIRST + start, 8), :] = result.reshape(8 * SUB, LANES)


def diffuse_edges(fields, coefs, keep_lower):
    row = lax.broadcasted_iota(jnp.int32, (8, SUB, LANES), 0)

    @pl.loop(1, PASSES + 1)
    def _(step):
        low, high = FIRST - HALO + step, FIRST + LATS - step
        lower = one_pass(fields, coefs, step, low)
        upper = one_pass(fields, coefs, step, high)
        lower = lower * jnp.where(row + low >= FIRST, 1.0, keep_lower)
        fields[step, tiles(low, 8), :] = lower.reshape(8 * SUB, LANES)
        fields[step, tiles(high, 8), :] = upper.reshape(8 * SUB, LANES)


def vertical_columns(band_ref, group_ref, out_ref):
    band = band_ref[...]
    group = group_ref[...]
    group = jnp.concatenate([group, group], axis=1)
    coefs = []
    for offset in range(-3, 4):
        coef = band[offset + 3 : offset + 4, :] + (1.0 if offset == 0 else 0.0)
        coef = jnp.concatenate([coef, coef], axis=1)
        ahead = group if offset == 0 else pltpu.roll(group, (-offset) % LANES, 1)
        coef = jnp.where(ahead == group, coef, 0.0)
        coefs.append(jnp.concatenate([coef, coef], axis=1))

    @pl.loop(0, 8)
    def _(part):
        shape = (32, 256)
        row = lax.broadcasted_iota(jnp.int32, shape, 0) + 32 * part
        col = lax.broadcasted_iota(jnp.int32, shape, 1)
        half, member, level = (row // 4) % 2, (row // 2) % 2, row % 2
        apart = 2 * (row // SUB) + level + 1024 * (2 * member + half) - col % 64 - 1024 * (col // 64)
        total = jnp.zeros(shape, F32)
        for offset in range(-3, 4):
            total = jnp.where(apart == offset, coefs[offset + 3], total)
        out_ref[pl.ds(pl.multiple_of(32 * part, 32), 32), :] = total


def two_parts(x):
    high = x.astype(jnp.bfloat16)
    return high, (x - high.astype(F32)).astype(jnp.bfloat16)


def split_matrix(matrix, out_ref):
    high, low = two_parts(matrix)
    out_ref[:, 0:256] = high
    out_ref[:, 256:512] = high
    out_ref[:, 512:768] = low


def product(matrix_ref, x):
    high, low = two_parts(x)
    return jnp.dot(matrix_ref[...], jnp.concatenate([high, low, high], axis=0), preferred_element_type=F32)


def kernel(
    control_hbm, members_hbm, east_hbm, south_hbm, innovation_hbm, huber_hbm, band_hbm, group_hbm,
    out,
    control, members, east_in, south_in, innovation, huber, band, group,
    east, west, south, fields, back_fields, east_edge, south_edge,
    gathered, lift, relay, full_matrix, lower_matrix, upper_matrix,
    term, parts, share,
    local_sems, edge_send, edge_recv, fwd_sems, sum_sems, share_sems,
    back_sems, block_sems, relay_sems, lev_ready, mem_ready,
):
    m, l, r = lax.axis_index("mem"), lax.axis_index("lev"), lax.axis_index("row")
    along, across = l // WIDE, lax.rem(l, WIDE)
    has_lower = (r + BLOCKS - 1) // BLOCKS
    has_upper = 1 - (r + 1) // BLOCKS
    low_edge = 1 - (l + LEVS - HALO) // LEVS
    high_edge = (l + HALO) // LEVS
    from_low = low_edge * has_lower
    from_high = high_edge * has_upper
    coefs = (east, west, south)

    def leader(row):
        return 28 - 24 * (row // 2)

    is_leader = jnp.where(l == leader(r), 1, 0)
    is_root = m // ROOT

    def remote(source, target, send, recv, **where):
        return pltpu.make_async_remote_copy(
            src_ref=source, dst_ref=target, send_sem=send, recv_sem=recv,
            device_id=where, device_id_type=MESH,
        )

    barrier = pltpu.get_barrier_semaphore()

    def tell(sem, **where):
        pl.semaphore_signal(sem, inc=1, device_id=where, device_id_type=MESH)

    @pl.when(r > 0)
    def _():
        tell(barrier, row=r - 1)

    @pl.when(r < BLOCKS - 1)
    def _():
        tell(barrier, row=r + 1)

    @pl.when(is_leader == 0)
    def _():
        tell(barrier, lev=leader(r))

    @pl.when(is_root == 0)
    def _():
        tell(barrier, mem=ROOT)

    @pl.when(from_low == 1)
    def _():
        tell(barrier, lev=leader(r - 1), row=r - 1)

    @pl.when(from_high == 1)
    def _():
        tell(barrier, lev=leader(r + 1), row=r + 1)

    loads = [
        pltpu.make_async_copy(source, target, local_sems.at[i])
        for i, (source, target) in enumerate([
            (control_hbm, control), (east_hbm, east_in), (south_hbm, south_in),
            (band_hbm, band), (group_hbm, group),
            (members_hbm, members), (innovation_hbm, innovation), (huber_hbm, huber),
        ])
    ]
    for load in loads:
        load.start()

    blank = jnp.zeros((HALO * SUB, LANES), F32)
    halo_refs = (east, west, south, fields.at[0], back_fields.at[0])

    @pl.when(r == 0)
    def _():
        for ref in halo_refs:
            ref[tiles(0, HALO), :] = blank

    @pl.when(r == BLOCKS - 1)
    def _():
        for ref in halo_refs:
            ref[tiles(FIRST + LATS, HALO), :] = blank

    loads[0].wait()
    for member in range(2):
        for level in range(2):
            own = control[member, level].astype(F32)
            for half in range(2):
                fields[0, pl.ds(SUB * FIRST + sublane(member, level, half), LATS, stride=SUB), :] = own[
                    :, half * LANES : (half + 1) * LANES
                ]
    loads[1].wait()
    loads[2].wait()

    pl.semaphore_wait(
        barrier,
        has_lower + has_upper + is_root * (MEMS - 1)
        + is_leader * (LEVS - 1 + HALO * (has_lower + has_upper)),
    )

    def edge_copies(side, row):
        edge = slice(0, HALO) if side == 0 else slice(LATS - HALO, LATS)
        first = FIRST if side == 0 else FIRST + LATS - HALO
        landing = FIRST + LATS if side == 0 else 0
        return [
            remote(fields.at[0, tiles(first, HALO), :], fields.at[0, tiles(landing, HALO), :],
                   edge_send.at[side, 0], edge_recv.at[side, 0], row=row),
            remote(east_in.at[:, edge, :], east_edge.at[side],
                   edge_send.at[side, 1], edge_recv.at[side, 1], row=row),
            remote(south_in.at[:, edge, :], south_edge.at[side],
                   edge_send.at[side, 2], edge_recv.at[side, 2], row=row),
        ]

    @pl.when(r > 0)
    def _():
        for copy in edge_copies(0, r - 1):
            copy.start()

    @pl.when(r < BLOCKS - 1)
    def _():
        for copy in edge_copies(1, r + 1):
            copy.start()

    @pl.when(is_leader == 1)
    def _():
        @pl.loop(1, LEVS)
        def _(i):
            tell(lev_ready, lev=lax.rem(l + i, LEVS))

        @pl.when(r < BLOCKS - 1)
        def _():
            @pl.loop(0, HALO)
            def _(i):
                tell(lev_ready, lev=i, row=r + 1)

        @pl.when(r > 0)
        def _():
            @pl.loop(0, HALO)
            def _(i):
                tell(lev_ready, lev=LEVS - HALO + i, row=r - 1)

    @pl.when(is_root == 1)
    def _():
        @pl.loop(0, MEMS - 1)
        def _(i):
            tell(mem_ready, mem=i)

    def place(target, value, level, first, count):
        for half in range(2):
            for member in range(2):
                target[pl.ds(SUB * first + sublane(member, level, half), count, stride=SUB), :] = value[
                    :, half * LANES : (half + 1) * LANES
                ]

    def set_west(first):
        value = east[tiles(first, 8), :].reshape(8, SUB, LANES)
        west[tiles(first, 8), :] = previous_longitude(value, lane_index()).reshape(8 * SUB, LANES)

    for level in range(2):
        place(east, east_in[level], level, FIRST, LATS)
        place(south, south_in[level], level, FIRST, LATS)
    for first in range(FIRST, FIRST + LATS, 8):
        set_west(first)
    diffuse_inside(fields, coefs)

    pl.semaphore_wait(lev_ready, 1 - is_leader + from_low + from_high)

    def send_latitudes(rows):
        for apart in FAR_FIRST:
            for row in rows:
                peer = WIDE * row + lax.rem(across + apart, WIDE)

                def send(peer=peer):
                    remote(fields.at[PASSES, tiles(FIRST + peer, 1), :], gathered.at[tiles(l, 1), :],
                           fwd_sems.at[0], fwd_sems.at[1], lev=peer).start()

                if apart:
                    send()
                else:
                    pl.when(along != row)(send)

    send_latitudes((1, 2))

    for load in loads[3:]:
        load.wait()
    vertical_columns(band, group, full_matrix)
    split_matrix(full_matrix[...], upper_matrix)
    split_matrix(full_matrix[...].T, lower_matrix)

    def take_edge(side, first):
        for copy in edge_copies(side, r):
            copy.wait_recv()
        for level in range(2):
            place(east, east_edge[side, level], level, first, HALO)
            place(south, south_edge[side, level], level, first, HALO)
        set_west(first)

    @pl.when(r < BLOCKS - 1)
    def _():
        take_edge(0, FIRST + LATS)

    @pl.when(r > 0)
    def _():
        take_edge(1, 0)

    keep_lower = has_lower.astype(F32)
    diffuse_edges(fields, coefs, keep_lower)
    send_latitudes((0, 3))

    gathered[tiles(l, 1), :] = fields[PASSES, tiles(FIRST + l, 1), :]
    everyone = remote(fields.at[PASSES, tiles(FIRST, LEVS - 1), :], gathered.at[tiles(0, LEVS - 1), :],
                      fwd_sems.at[0], fwd_sems.at[1], lev=l)
    everyone.wait_recv()

    filtered = product(lower_matrix, gathered[...])

    def member_columns(member, half):
        return members[member, :, half * LANES : (half + 1) * LANES].astype(F32)

    for half in range(2):
        term[half] = sum(
            member_columns(member, half) * filtered[64 * (2 * member + half) : 64 * (2 * member + half + 1)]
            for member in range(2)
        )

    roots = (ROOT, 0)
    orders = ((0, 6, 1, 5, 2, 4, 3), (1, 7, 2, 6, 3, 5, 4))

    def term_copy(half):
        return remote(term.at[half], parts.at[m - half, half], sum_sems.at[0, half], sum_sems.at[1, half],
                      mem=roots[half])

    def share_copy(half, mem):
        return remote(share.at[half], share.at[half], share_sems.at[0, half], share_sems.at[1, half], mem=mem)

    def rest(half, sems):
        others = parts.at[pl.ds(0, MEMS - 1), half]
        return remote(others, others, sems.at[0, half], sems.at[1, half], mem=m)

    def gather_half(half):
        rest(half, sum_sems).wait_recv()
        values = [parts[i, half] for i in range(MEMS - 1)]
        values.insert(roots[half], term[half])
        increment = values[0]
        for value in values[1:]:
            increment = increment + value
        lanes = slice(half * LANES, (half + 1) * LANES)
        residual = increment - innovation[:, lanes]
        scale = HUBER / jnp.maximum(jnp.abs(residual), HUBER)
        share[half] = jnp.where(huber[:, lanes] == 1, scale, 1.0) * residual
        for mem in orders[half]:
            share_copy(half, mem).start()

    @pl.when(is_root == 0)
    def _():
        pl.semaphore_wait(mem_ready, 1)
        term_copy(0).start()

    @pl.when(m > 0)
    def _():
        term_copy(1).start()

    @pl.when(is_root == 1)
    def _():
        gather_half(0)
        share_copy(1, 0).wait_recv()

    @pl.when(m == 0)
    def _():
        gather_half(1)
        share_copy(0, 0).wait_recv()

    @pl.when((m > 0) & (is_root == 0))
    def _():
        for half in range(2):
            share_copy(half, 0).wait_recv()

    adjoint = jnp.concatenate(
        [member_columns(member, half) * share[half] for member in range(2) for half in range(2)], axis=0
    )
    lift[...] = product(upper_matrix, adjoint)

    def block_copy(side, position, row):
        return remote(lift.at[tiles(WIDE * position, WIDE), :], relay.at[side],
                      block_sems.at[side, 0], block_sems.at[side, 1],
                      lev=WIDE * position + across, row=row)

    def landing(side):
        return FIRST + LATS if side == 0 else 0

    def direct_copy(side, peer, row):
        return remote(lift.at[tiles(peer, 1), :], back_fields.at[0, tiles(landing(side) + across, 1), :],
                      block_sems.at[side, 2], relay_sems.at[side, 1], lev=peer, row=row)

    def send_edges(side, positions, row):
        for apart in FAR_FIRST:
            for position in range(DIRECT):
                direct_copy(side, WIDE * position + lax.rem(across + apart, WIDE), row).start()
        for position in positions:
            block_copy(side, position, row).start()

    @pl.when(from_low == 1)
    def _():
        send_edges(0, range(DIRECT, 4), r - 1)

    @pl.when(from_high == 1)
    def _():
        send_edges(1, range(3, DIRECT - 1, -1), r + 1)

    for apart in FAR_FIRST:
        for turn in range(4):
            if apart or turn:
                peer = WIDE * lax.rem(along + turn, 4) + lax.rem(across + apart, WIDE)
                remote(lift.at[tiles(peer, 1), :], back_fields.at[0, tiles(FIRST + l, 1), :],
                       back_sems.at[0], back_sems.at[1], lev=peer).start()

    back_fields[0, tiles(FIRST + l, 1), :] = lift[tiles(l, 1), :]

    def hand_on(side):
        block_copy(side, along, r).wait_recv()
        for apart in FAR_FIRST[:-1]:
            column = lax.rem(across + apart, WIDE)
            remote(relay.at[side, tiles(column, 1), :],
                   back_fields.at[0, tiles(landing(side) + across, 1), :],
                   relay_sems.at[side, 0], relay_sems.at[side, 1], lev=WIDE * along + column).start()
        back_fields[0, tiles(landing(side) + across, 1), :] = relay[side, tiles(across, 1), :]

    def handed(side, count):
        return remote(relay.at[side, tiles(0, count), :],
                      back_fields.at[0, tiles(landing(side), count), :],
                      relay_sems.at[side, 0], relay_sems.at[side, 1], lev=l)

    @pl.when((r > 0) & (along >= DIRECT))
    def _():
        hand_on(1)

    @pl.when((r < BLOCKS - 1) & (along >= DIRECT))
    def _():
        hand_on(0)

    columns = remote(lift.at[tiles(0, LEVS - 1), :], back_fields.at[0, tiles(FIRST, LEVS - 1), :],
                     back_sems.at[0], back_sems.at[1], lev=l)
    columns.wait_recv()
    diffuse_inside(back_fields, coefs)

    def halo_arrived(side):
        @pl.when(along >= DIRECT)
        def _():
            handed(side, WIDE - 1).wait_recv()

        @pl.when(along < DIRECT)
        def _():
            handed(side, WIDE).wait_recv()

    @pl.when(r > 0)
    def _():
        halo_arrived(1)

    @pl.when(r < BLOCKS - 1)
    def _():
        halo_arrived(0)

    diffuse_edges(back_fields, coefs, keep_lower)

    for member in range(2):
        for level in range(2):
            for half in range(2):
                lanes = slice(half * LANES, (half + 1) * LANES)
                smooth = back_fields[
                    PASSES, pl.ds(SUB * FIRST + sublane(member, level, half), LATS, stride=SUB), :
                ]
                out[member, level, :, lanes] = control[member, level, :, lanes].astype(F32) + smooth


    @pl.when(r > 0)
    def _():
        for copy in edge_copies(0, r - 1):
            copy.wait_send()

        @pl.when(along >= DIRECT)
        def _():
            handed(1, WIDE - 1).wait_send()

    @pl.when(r < BLOCKS - 1)
    def _():
        for copy in edge_copies(1, r + 1):
            copy.wait_send()

        @pl.when(along >= DIRECT)
        def _():
            handed(0, WIDE - 1).wait_send()

    everyone.wait_send()

    @pl.when(is_root == 0)
    def _():
        term_copy(0).wait_send()

    @pl.when(m > 0)
    def _():
        term_copy(1).wait_send()

    @pl.when(is_root == 1)
    def _():
        rest(0, share_sems).wait_send()

    @pl.when(m == 0)
    def _():
        rest(1, share_sems).wait_send()

    def edges_sent(side):
        for way, count in ((0, LEVS - DIRECT * WIDE), (2, DIRECT * WIDE)):
            remote(lift.at[tiles(0, count), :], lift.at[tiles(0, count), :],
                   block_sems.at[side, way], block_sems.at[side, 1], lev=l).wait_send()

    @pl.when(from_low == 1)
    def _():
        edges_sent(0)

    @pl.when(from_high == 1)
    def _():
        edges_sent(1)

    columns.wait_send()


def per_device(
    control, members, east_coef, south_coef, innovation, huber_class, band, level_group_index
):
    hbm = pl.BlockSpec(memory_space=pl.ANY)
    dma = pltpu.SemaphoreType.DMA
    group = level_group_index.reshape(1, -1)
    rows = pltpu.VMEM((SUB * ROWS, LANES), F32)
    return pl.pallas_call(
        kernel,
        out_shape=jax.ShapeDtypeStruct(control.shape, F32),
        in_specs=[hbm] * 8,
        out_specs=pl.BlockSpec(memory_space=pltpu.VMEM),
        scratch_shapes=[
            pltpu.VMEM(control.shape, jnp.bfloat16),
            pltpu.VMEM(members.shape, jnp.bfloat16),
            pltpu.VMEM(east_coef.shape, F32),
            pltpu.VMEM(south_coef.shape, F32),
            pltpu.VMEM(innovation.shape, F32),
            pltpu.VMEM(huber_class.shape, jnp.int32),
            pltpu.VMEM(band.shape, F32),
            pltpu.VMEM(group.shape, jnp.int32),
            rows,
            rows,
            rows,
            pltpu.VMEM((PASSES + 1, SUB * ROWS, LANES), F32),
            pltpu.VMEM((PASSES + 1, SUB * ROWS, LANES), F32),
            pltpu.VMEM((2, 2, HALO, 2 * LANES), F32),
            pltpu.VMEM((2, 2, HALO, 2 * LANES), F32),
            pltpu.VMEM((SUB * LEVS, LANES), F32),
            pltpu.VMEM((SUB * LEVS, LANES), F32),
            pltpu.VMEM((2, SUB * WIDE, LANES), F32),
            pltpu.VMEM((256, 256), F32),
            pltpu.VMEM((256, 768), jnp.bfloat16),
            pltpu.VMEM((256, 768), jnp.bfloat16),
            pltpu.VMEM((2, 64, LANES), F32),
            pltpu.VMEM((MEMS - 1, 2, 64, LANES), F32),
            pltpu.VMEM((2, 64, LANES), F32),
            dma((8,)),
            dma((2, 3)),
            dma((2, 3)),
            dma((2,)),
            dma((2, 2)),
            dma((2, 2)),
            dma((2,)),
            dma((2, 3)),
            dma((2, 2)),
            pltpu.SemaphoreType.REGULAR,
            pltpu.SemaphoreType.REGULAR,
        ],
        compiler_params=pltpu.CompilerParams(collective_id=0, has_side_effects=True, vmem_limit_bytes=16 << 20),
        name="hybrid_gradient",
    )(*[pltpu.with_memory_space_constraint(x, pltpu.HBM) for x in (control, members, east_coef, south_coef, innovation, huber_class, band, group)])


def solution(mesh):
    placed = (
        P("mem", "lev", "row", None),
        P("mem", None, ("row", "lev")),
        P("lev", "row", None),
        P("lev", "row", None),
        P(None, ("row", "lev")),
        P(None, ("row", "lev")),
        P(),
        P(),
    )
    return jax.shard_map(
        per_device,
        mesh=mesh,
        in_specs=placed,
        out_specs=P("mem", "lev", "row", None),
        check_vma=False,
    )
```

```python
import jax
import jax.numpy as jnp
from jax import lax
from jax.experimental import pallas as pl
from jax.experimental.pallas import tpu as pltpu
from jax.sharding import PartitionSpec as P

PASSES = 8
HUBER = 1.0
MESH = pl.DeviceIdType.MESH
F32 = jnp.float32

LANES = 128
SUB = 8
LATS = 32
HALO = 8
FIRST = HALO
ROWS = LATS + 2 * HALO
LEVS = 32
WIDE = 8
MEMS = 8
ROOT = MEMS - 1
DIRECT = 1
BLOCKS = 4
FAR_FIRST = (4, 3, 5, 2, 6, 1, 7, 0)


def tiles(start, count):
    if isinstance(start, int):
        return pl.ds(SUB * start, SUB * count)
    return pl.ds(pl.multiple_of(SUB * start, SUB), SUB * count)


def sublane(member, level, half):
    return 4 * half + 2 * member + level


def next_longitude(x, lane):
    turned = pltpu.roll(x, LANES - 1, 2)
    return jnp.where(lane == LANES - 1, pltpu.roll(turned, 4, 1), turned)


def previous_longitude(x, lane):
    turned = pltpu.roll(x, 1, 2)
    return jnp.where(lane == 0, pltpu.roll(turned, 4, 1), turned)


def lane_index():
    return lax.broadcasted_iota(jnp.int32, (8, SUB, LANES), 2)


def one_pass(fields, coefs, step, start):
    east, west, south = coefs
    lane = lane_index()

    def field(row):
        return fields[step - 1, tiles(row, 8), :].reshape(8, SUB, LANES)

    def coef(ref, row):
        return ref[tiles(row, 8), :].reshape(8, SUB, LANES)

    center = field(start)
    flux_x = coef(east, start) * (next_longitude(center, lane) - center)
    flux_west = coef(west, start) * (center - previous_longitude(center, lane))
    flux_in = coef(south, start) * (center - field(start - 1))
    flux_out = coef(south, start + 1) * (field(start + 1) - center)
    return center + flux_x - flux_west + flux_out - flux_in


def diffuse_inside(fields, coefs):
    for step in range(1, PASSES + 1):
        starts = list(range(step, 24 - step, 8)) + [24 - step]
        for start in starts:
            result = one_pass(fields, coefs, step, FIRST + start)
            fields[step, tiles(FIRST + start, 8), :] = result.reshape(8 * SUB, LANES)


def diffuse_edges(fields, coefs, keep_lower):
    row = lax.broadcasted_iota(jnp.int32, (8, SUB, LANES), 0)

    @pl.loop(1, PASSES + 1)
    def _(step):
        low, high = FIRST - HALO + step, FIRST + LATS - step
        lower = one_pass(fields, coefs, step, low)
        upper = one_pass(fields, coefs, step, high)
        lower = lower * jnp.where(row + low >= FIRST, 1.0, keep_lower)
        fields[step, tiles(low, 8), :] = lower.reshape(8 * SUB, LANES)
        fields[step, tiles(high, 8), :] = upper.reshape(8 * SUB, LANES)


def vertical_columns(band_ref, group_ref, out_ref):
    band = band_ref[...]
    group = group_ref[...]
    group = jnp.concatenate([group, group], axis=1)
    coefs = []
    for offset in range(-3, 4):
        coef = band[offset + 3 : offset + 4, :] + (1.0 if offset == 0 else 0.0)
        coef = jnp.concatenate([coef, coef], axis=1)
        ahead = group if offset == 0 else pltpu.roll(group, (-offset) % LANES, 1)
        coef = jnp.where(ahead == group, coef, 0.0)
        coefs.append(jnp.concatenate([coef, coef], axis=1))

    @pl.loop(0, 8)
    def _(part):
        shape = (32, 256)
        row = lax.broadcasted_iota(jnp.int32, shape, 0) + 32 * part
        col = lax.broadcasted_iota(jnp.int32, shape, 1)
        half, member, level = (row // 4) % 2, (row // 2) % 2, row % 2
        apart = 2 * (row // SUB) + level + 1024 * (2 * member + half) - col % 64 - 1024 * (col // 64)
        total = jnp.zeros(shape, F32)
        for offset in range(-3, 4):
            total = jnp.where(apart == offset, coefs[offset + 3], total)
        out_ref[pl.ds(pl.multiple_of(32 * part, 32), 32), :] = total


def two_parts(x):
    high = x.astype(jnp.bfloat16)
    return high, (x - high.astype(F32)).astype(jnp.bfloat16)


def split_matrix(matrix, out_ref):
    high, low = two_parts(matrix)
    out_ref[:, 0:256] = high
    out_ref[:, 256:512] = high
    out_ref[:, 512:768] = low


def product(matrix_ref, x):
    high, low = two_parts(x)
    return jnp.dot(matrix_ref[...], jnp.concatenate([high, low, high], axis=0), preferred_element_type=F32)


def kernel(
    control_hbm, members_hbm, east_hbm, south_hbm, innovation_hbm, huber_hbm, band_hbm, group_hbm,
    out,
    control, members, east_in, south_in, innovation, huber, band, group,
    east, west, south, fields, back_fields, east_edge, south_edge,
    gathered, lift, relay, full_matrix, lower_matrix, upper_matrix,
    term, parts, share,
    local_sems, edge_send, edge_recv, fwd_sems, sum_sems, share_sems,
    back_sems, block_sems, relay_sems, pair_sems, lev_ready, mem_ready,
):
    m, l, r = lax.axis_index("mem"), lax.axis_index("lev"), lax.axis_index("row")
    along, across = l // WIDE, lax.rem(l, WIDE)
    has_lower = (r + BLOCKS - 1) // BLOCKS
    has_upper = 1 - (r + 1) // BLOCKS
    low_edge = 1 - (l + LEVS - HALO) // LEVS
    high_edge = (l + HALO) // LEVS
    from_low = low_edge * has_lower
    from_high = high_edge * has_upper
    parity = lax.rem(r, 2)
    pair_along = 3 * (1 - parity)
    in_pair_rows = jnp.where(along == pair_along, 1, 0)
    coefs = (east, west, south)

    def leader(row):
        return 28 - 24 * (row // 2)

    is_leader = jnp.where(l == leader(r), 1, 0)
    is_root = m // ROOT

    def remote(source, target, send, recv, **where):
        return pltpu.make_async_remote_copy(
            src_ref=source, dst_ref=target, send_sem=send, recv_sem=recv,
            device_id=where, device_id_type=MESH,
        )

    barrier = pltpu.get_barrier_semaphore()

    def tell(sem, **where):
        pl.semaphore_signal(sem, inc=1, device_id=where, device_id_type=MESH)

    @pl.when(r > 0)
    def _():
        tell(barrier, row=r - 1)

    @pl.when(r < BLOCKS - 1)
    def _():
        tell(barrier, row=r + 1)

    @pl.when(is_leader == 0)
    def _():
        tell(barrier, lev=leader(r))

    @pl.when(is_root == 0)
    def _():
        tell(barrier, mem=ROOT)

    @pl.when(from_low == 1)
    def _():
        tell(barrier, lev=leader(r - 1), row=r - 1)

    @pl.when(from_high == 1)
    def _():
        tell(barrier, lev=leader(r + 1), row=r + 1)

    loads = [
        pltpu.make_async_copy(source, target, local_sems.at[i])
        for i, (source, target) in enumerate([
            (control_hbm, control), (east_hbm, east_in), (south_hbm, south_in),
            (band_hbm, band), (group_hbm, group),
            (members_hbm, members), (innovation_hbm, innovation), (huber_hbm, huber),
        ])
    ]
    for load in loads:
        load.start()

    blank = jnp.zeros((HALO * SUB, LANES), F32)
    halo_refs = (east, west, south, fields.at[0], back_fields.at[0])

    @pl.when(r == 0)
    def _():
        for ref in halo_refs:
            ref[tiles(0, HALO), :] = blank

    @pl.when(r == BLOCKS - 1)
    def _():
        for ref in halo_refs:
            ref[tiles(FIRST + LATS, HALO), :] = blank

    loads[0].wait()
    for member in range(2):
        for level in range(2):
            own = control[member, level].astype(F32)
            for half in range(2):
                fields[0, pl.ds(SUB * FIRST + sublane(member, level, half), LATS, stride=SUB), :] = own[
                    :, half * LANES : (half + 1) * LANES
                ]
    loads[1].wait()
    loads[2].wait()

    pl.semaphore_wait(
        barrier,
        has_lower + has_upper + is_root * (MEMS - 1)
        + is_leader * (LEVS - 1 + HALO * (has_lower + has_upper)),
    )

    def edge_copies(side, row):
        edge = slice(0, HALO) if side == 0 else slice(LATS - HALO, LATS)
        first = FIRST if side == 0 else FIRST + LATS - HALO
        landing = FIRST + LATS if side == 0 else 0
        return [
            remote(fields.at[0, tiles(first, HALO), :], fields.at[0, tiles(landing, HALO), :],
                   edge_send.at[side, 0], edge_recv.at[side, 0], row=row),
            remote(east_in.at[:, edge, :], east_edge.at[side],
                   edge_send.at[side, 1], edge_recv.at[side, 1], row=row),
            remote(south_in.at[:, edge, :], south_edge.at[side],
                   edge_send.at[side, 2], edge_recv.at[side, 2], row=row),
        ]

    @pl.when(r > 0)
    def _():
        for copy in edge_copies(0, r - 1):
            copy.start()

    @pl.when(r < BLOCKS - 1)
    def _():
        for copy in edge_copies(1, r + 1):
            copy.start()

    @pl.when(is_leader == 1)
    def _():
        @pl.loop(1, LEVS)
        def _(i):
            tell(lev_ready, lev=lax.rem(l + i, LEVS))

        @pl.when(r < BLOCKS - 1)
        def _():
            @pl.loop(0, HALO)
            def _(i):
                tell(lev_ready, lev=i, row=r + 1)

        @pl.when(r > 0)
        def _():
            @pl.loop(0, HALO)
            def _(i):
                tell(lev_ready, lev=LEVS - HALO + i, row=r - 1)

    @pl.when(is_root == 1)
    def _():
        @pl.loop(0, MEMS - 1)
        def _(i):
            tell(mem_ready, mem=i)

    def place(target, value, level, first, count):
        for half in range(2):
            for member in range(2):
                target[pl.ds(SUB * first + sublane(member, level, half), count, stride=SUB), :] = value[
                    :, half * LANES : (half + 1) * LANES
                ]

    def set_west(first):
        value = east[tiles(first, 8), :].reshape(8, SUB, LANES)
        west[tiles(first, 8), :] = previous_longitude(value, lane_index()).reshape(8 * SUB, LANES)

    for level in range(2):
        place(east, east_in[level], level, FIRST, LATS)
        place(south, south_in[level], level, FIRST, LATS)
    for first in range(FIRST, FIRST + LATS, 8):
        set_west(first)
    diffuse_inside(fields, coefs)

    pl.semaphore_wait(lev_ready, 1 - is_leader + from_low + from_high)

    def send_latitudes(rows):
        for apart in FAR_FIRST:
            for row in rows:
                peer = WIDE * row + lax.rem(across + apart, WIDE)

                def send(peer=peer):
                    remote(fields.at[PASSES, tiles(FIRST + peer, 1), :], gathered.at[tiles(l, 1), :],
                           fwd_sems.at[0], fwd_sems.at[1], lev=peer).start()

                if apart:
                    send()
                else:
                    pl.when(along != row)(send)

    send_latitudes((1, 2))

    for load in loads[3:]:
        load.wait()
    vertical_columns(band, group, full_matrix)
    split_matrix(full_matrix[...], upper_matrix)
    split_matrix(full_matrix[...].T, lower_matrix)

    def take_edge(side, first):
        for copy in edge_copies(side, r):
            copy.wait_recv()
        for level in range(2):
            place(east, east_edge[side, level], level, first, HALO)
            place(south, south_edge[side, level], level, first, HALO)
        set_west(first)

    @pl.when(r < BLOCKS - 1)
    def _():
        take_edge(0, FIRST + LATS)

    @pl.when(r > 0)
    def _():
        take_edge(1, 0)

    keep_lower = has_lower.astype(F32)
    diffuse_edges(fields, coefs, keep_lower)
    send_latitudes((3, 0))

    gathered[tiles(l, 1), :] = fields[PASSES, tiles(FIRST + l, 1), :]
    everyone = remote(fields.at[PASSES, tiles(FIRST, LEVS - 1), :], gathered.at[tiles(0, LEVS - 1), :],
                      fwd_sems.at[0], fwd_sems.at[1], lev=l)
    everyone.wait_recv()

    filtered = product(lower_matrix, gathered[...])

    def member_columns(member, half):
        return members[member, :, half * LANES : (half + 1) * LANES].astype(F32)

    for half in range(2):
        term[half] = sum(
            member_columns(member, half) * filtered[64 * (2 * member + half) : 64 * (2 * member + half + 1)]
            for member in range(2)
        )

    roots = (ROOT, 0)
    orders = ((0, 6, 1, 5, 2, 4, 3), (1, 7, 2, 6, 3, 5, 4))

    def term_copy(half):
        return remote(term.at[half], parts.at[m - half, half], sum_sems.at[0, half], sum_sems.at[1, half],
                      mem=roots[half])

    def share_copy(half, mem):
        return remote(share.at[half], share.at[half], share_sems.at[0, half], share_sems.at[1, half], mem=mem)

    def rest(half, sems):
        others = parts.at[pl.ds(0, MEMS - 1), half]
        return remote(others, others, sems.at[0, half], sems.at[1, half], mem=m)

    def gather_half(half):
        rest(half, sum_sems).wait_recv()
        values = [parts[i, half] for i in range(MEMS - 1)]
        values.insert(roots[half], term[half])
        increment = values[0]
        for value in values[1:]:
            increment = increment + value
        lanes = slice(half * LANES, (half + 1) * LANES)
        residual = increment - innovation[:, lanes]
        scale = HUBER / jnp.maximum(jnp.abs(residual), HUBER)
        share[half] = jnp.where(huber[:, lanes] == 1, scale, 1.0) * residual
        for mem in orders[half]:
            share_copy(half, mem).start()

    @pl.when(is_root == 0)
    def _():
        pl.semaphore_wait(mem_ready, 1)
        term_copy(0).start()

    @pl.when(m > 0)
    def _():
        term_copy(1).start()

    @pl.when(is_root == 1)
    def _():
        gather_half(0)
        share_copy(1, 0).wait_recv()

    @pl.when(m == 0)
    def _():
        gather_half(1)
        share_copy(0, 0).wait_recv()

    @pl.when((m > 0) & (is_root == 0))
    def _():
        for half in range(2):
            share_copy(half, 0).wait_recv()

    adjoint = jnp.concatenate(
        [member_columns(member, half) * share[half] for member in range(2) for half in range(2)], axis=0
    )
    lift[...] = product(upper_matrix, adjoint)

    def block_copy(side, position, row):
        return remote(lift.at[tiles(WIDE * position, WIDE), :], relay.at[side],
                      block_sems.at[side, 0], block_sems.at[side, 1],
                      lev=WIDE * position + across, row=row)

    def landing(side):
        return FIRST + LATS if side == 0 else 0

    def direct_copy(side, peer, row):
        return remote(lift.at[tiles(peer, 1), :], back_fields.at[0, tiles(landing(side) + across, 1), :],
                      block_sems.at[side, 2], relay_sems.at[side, 1], lev=peer, row=row)

    def send_edges(side, positions, row):
        for position in range(DIRECT):
            for apart in FAR_FIRST:
                direct_copy(side, WIDE * position + lax.rem(across + apart, WIDE), row).start()
        for position in positions:
            block_copy(side, position, row).start()

    @pl.when((r == 2) & (low_edge == 1))
    def _():
        send_edges(0, range(DIRECT, 4), 1)

    @pl.when((r == 1) & (high_edge == 1))
    def _():
        send_edges(1, range(3, DIRECT - 1, -1), 2)

    for apart in FAR_FIRST:
        for turn in range(4):
            if apart or turn:
                peer = WIDE * lax.rem(along + turn, 4) + lax.rem(across + apart, WIDE)
                remote(lift.at[tiles(peer, 1), :], back_fields.at[0, tiles(FIRST + l, 1), :],
                       back_sems.at[0], back_sems.at[2 - in_pair_rows], lev=peer).start()

    back_fields[0, tiles(FIRST + l, 1), :] = lift[tiles(l, 1), :]

    def hand_on(side):
        block_copy(side, along, r).wait_recv()
        for apart in FAR_FIRST[:-1]:
            column = lax.rem(across + apart, WIDE)
            remote(relay.at[side, tiles(column, 1), :],
                   back_fields.at[0, tiles(landing(side) + across, 1), :],
                   relay_sems.at[side, 0], relay_sems.at[side, 1], lev=WIDE * along + column).start()
        back_fields[0, tiles(landing(side) + across, 1), :] = relay[side, tiles(across, 1), :]

    def handed(side, count):
        return remote(relay.at[side, tiles(0, count), :],
                      back_fields.at[0, tiles(landing(side), count), :],
                      relay_sems.at[side, 0], relay_sems.at[side, 1], lev=l)

    @pl.when((r == 2) & (along >= DIRECT))
    def _():
        hand_on(1)

    @pl.when((r == 1) & (along >= DIRECT))
    def _():
        hand_on(0)

    def columns(group, count):
        return remote(lift.at[tiles(0, count), :], back_fields.at[0, tiles(FIRST, count), :],
                      back_sems.at[0], back_sems.at[group], lev=l)

    def to_pair(source, target, row):
        return remote(back_fields.at[0, tiles(source, HALO), :], back_fields.at[0, tiles(target, HALO), :],
                      pair_sems.at[0], pair_sems.at[1], row=row)

    def pair_copy(even, row):
        if even:
            return to_pair(FIRST + LATS - HALO, 0, row)
        return to_pair(FIRST, FIRST + LATS, row)

    @pl.when(in_pair_rows == 1)
    def _():
        columns(1, WIDE - 1).wait_recv()

    @pl.when(in_pair_rows == 0)
    def _():
        columns(1, WIDE).wait_recv()

    @pl.when(parity == 0)
    def _():
        pair_copy(True, r + 1).start()

    @pl.when(parity == 1)
    def _():
        pair_copy(False, r - 1).start()

    @pl.when(in_pair_rows == 1)
    def _():
        columns(2, LEVS - WIDE).wait_recv()

    @pl.when(in_pair_rows == 0)
    def _():
        columns(2, LEVS - WIDE - 1).wait_recv()

    diffuse_inside(back_fields, coefs)

    @pl.when(parity == 0)
    def _():
        pair_copy(False, r + 1).wait_recv()

    @pl.when(parity == 1)
    def _():
        pair_copy(True, r - 1).wait_recv()

    def halo_arrived(side):
        @pl.when(along >= DIRECT)
        def _():
            handed(side, WIDE - 1).wait_recv()

        @pl.when(along < DIRECT)
        def _():
            handed(side, WIDE).wait_recv()

    @pl.when(r == 2)
    def _():
        halo_arrived(1)

    @pl.when(r == 1)
    def _():
        halo_arrived(0)

    diffuse_edges(back_fields, coefs, keep_lower)

    for member in range(2):
        for level in range(2):
            for half in range(2):
                lanes = slice(half * LANES, (half + 1) * LANES)
                smooth = back_fields[
                    PASSES, pl.ds(SUB * FIRST + sublane(member, level, half), LATS, stride=SUB), :
                ]
                out[member, level, :, lanes] = control[member, level, :, lanes].astype(F32) + smooth


    @pl.when(r > 0)
    def _():
        for copy in edge_copies(0, r - 1):
            copy.wait_send()

    @pl.when(r < BLOCKS - 1)
    def _():
        for copy in edge_copies(1, r + 1):
            copy.wait_send()

    @pl.when((r == 2) & (along >= DIRECT))
    def _():
        handed(1, WIDE - 1).wait_send()

    @pl.when((r == 1) & (along >= DIRECT))
    def _():
        handed(0, WIDE - 1).wait_send()

    @pl.when(parity == 0)
    def _():
        pair_copy(True, r + 1).wait_send()

    @pl.when(parity == 1)
    def _():
        pair_copy(False, r - 1).wait_send()

    everyone.wait_send()

    @pl.when(is_root == 0)
    def _():
        term_copy(0).wait_send()

    @pl.when(m > 0)
    def _():
        term_copy(1).wait_send()

    @pl.when(is_root == 1)
    def _():
        rest(0, share_sems).wait_send()

    @pl.when(m == 0)
    def _():
        rest(1, share_sems).wait_send()

    def edges_sent(side):
        for way, count in ((0, LEVS - DIRECT * WIDE), (2, DIRECT * WIDE)):
            remote(lift.at[tiles(0, count), :], lift.at[tiles(0, count), :],
                   block_sems.at[side, way], block_sems.at[side, 1], lev=l).wait_send()

    @pl.when((r == 2) & (low_edge == 1))
    def _():
        edges_sent(0)

    @pl.when((r == 1) & (high_edge == 1))
    def _():
        edges_sent(1)

    columns(1, LEVS - 1).wait_send()


def per_device(
    control, members, east_coef, south_coef, innovation, huber_class, band, level_group_index
):
    hbm = pl.BlockSpec(memory_space=pl.ANY)
    dma = pltpu.SemaphoreType.DMA
    group = level_group_index.reshape(1, -1)
    rows = pltpu.VMEM((SUB * ROWS, LANES), F32)
    return pl.pallas_call(
        kernel,
        out_shape=jax.ShapeDtypeStruct(control.shape, F32),
        in_specs=[hbm] * 8,
        out_specs=pl.BlockSpec(memory_space=pltpu.VMEM),
        scratch_shapes=[
            pltpu.VMEM(control.shape, jnp.bfloat16),
            pltpu.VMEM(members.shape, jnp.bfloat16),
            pltpu.VMEM(east_coef.shape, F32),
            pltpu.VMEM(south_coef.shape, F32),
            pltpu.VMEM(innovation.shape, F32),
            pltpu.VMEM(huber_class.shape, jnp.int32),
            pltpu.VMEM(band.shape, F32),
            pltpu.VMEM(group.shape, jnp.int32),
            rows,
            rows,
            rows,
            pltpu.VMEM((PASSES + 1, SUB * ROWS, LANES), F32),
            pltpu.VMEM((PASSES + 1, SUB * ROWS, LANES), F32),
            pltpu.VMEM((2, 2, HALO, 2 * LANES), F32),
            pltpu.VMEM((2, 2, HALO, 2 * LANES), F32),
            pltpu.VMEM((SUB * LEVS, LANES), F32),
            pltpu.VMEM((SUB * LEVS, LANES), F32),
            pltpu.VMEM((2, SUB * WIDE, LANES), F32),
            pltpu.VMEM((256, 256), F32),
            pltpu.VMEM((256, 768), jnp.bfloat16),
            pltpu.VMEM((256, 768), jnp.bfloat16),
            pltpu.VMEM((2, 64, LANES), F32),
            pltpu.VMEM((MEMS - 1, 2, 64, LANES), F32),
            pltpu.VMEM((2, 64, LANES), F32),
            dma((8,)),
            dma((2, 3)),
            dma((2, 3)),
            dma((2,)),
            dma((2, 2)),
            dma((2, 2)),
            dma((3,)),
            dma((2, 3)),
            dma((2, 2)),
            dma((2,)),
            pltpu.SemaphoreType.REGULAR,
            pltpu.SemaphoreType.REGULAR,
        ],
        compiler_params=pltpu.CompilerParams(collective_id=0, has_side_effects=True, vmem_limit_bytes=16 << 20),
        name="hybrid_gradient",
    )(*[pltpu.with_memory_space_constraint(x, pltpu.HBM) for x in (control, members, east_coef, south_coef, innovation, huber_class, band, group)])


def solution(mesh):
    placed = (
        P("mem", "lev", "row", None),
        P("mem", None, ("row", "lev")),
        P("lev", "row", None),
        P("lev", "row", None),
        P(None, ("row", "lev")),
        P(None, ("row", "lev")),
        P(),
        P(),
    )
    return jax.shard_map(
        per_device,
        mesh=mesh,
        in_specs=placed,
        out_specs=P("mem", "lev", "row", None),
        check_vma=False,
    )
```

```python
import jax
import jax.numpy as jnp
from jax import lax
from jax.experimental import pallas as pl
from jax.experimental.pallas import tpu as pltpu
from jax.sharding import PartitionSpec as P

PASSES = 8
HUBER = 1.0
MESH = pl.DeviceIdType.MESH
F32 = jnp.float32

LANES = 128
SUB = 8
LATS = 32
HALO = 8
FIRST = HALO
ROWS = LATS + 2 * HALO
LEVS = 32
WIDE = 8
MEMS = 8
ROOT = MEMS - 1
DIRECT = 1
BLOCKS = 4
FAR_FIRST = (4, 3, 5, 2, 6, 1, 7, 0)


def tiles(start, count):
    if isinstance(start, int):
        return pl.ds(SUB * start, SUB * count)
    return pl.ds(pl.multiple_of(SUB * start, SUB), SUB * count)


def sublane(member, level, half):
    return 4 * half + 2 * member + level


def next_longitude(x, lane):
    turned = pltpu.roll(x, LANES - 1, 2)
    return jnp.where(lane == LANES - 1, pltpu.roll(turned, 4, 1), turned)


def previous_longitude(x, lane):
    turned = pltpu.roll(x, 1, 2)
    return jnp.where(lane == 0, pltpu.roll(turned, 4, 1), turned)


def lane_index():
    return lax.broadcasted_iota(jnp.int32, (8, SUB, LANES), 2)


def one_pass(fields, coefs, step, start):
    east, west, south = coefs
    lane = lane_index()

    def field(row):
        return fields[step - 1, tiles(row, 8), :].reshape(8, SUB, LANES)

    def coef(ref, row):
        return ref[tiles(row, 8), :].reshape(8, SUB, LANES)

    center = field(start)
    flux_x = coef(east, start) * (next_longitude(center, lane) - center)
    flux_west = coef(west, start) * (center - previous_longitude(center, lane))
    flux_in = coef(south, start) * (center - field(start - 1))
    flux_out = coef(south, start + 1) * (field(start + 1) - center)
    return center + flux_x - flux_west + flux_out - flux_in


def diffuse_inside(fields, coefs):
    for step in range(1, PASSES + 1):
        starts = list(range(step, 24 - step, 8)) + [24 - step]
        for start in starts:
            result = one_pass(fields, coefs, step, FIRST + start)
            fields[step, tiles(FIRST + start, 8), :] = result.reshape(8 * SUB, LANES)


def diffuse_edges(fields, coefs, keep_lower):
    row = lax.broadcasted_iota(jnp.int32, (8, SUB, LANES), 0)

    @pl.loop(1, PASSES + 1)
    def _(step):
        low, high = FIRST - HALO + step, FIRST + LATS - step
        lower = one_pass(fields, coefs, step, low)
        upper = one_pass(fields, coefs, step, high)
        lower = lower * jnp.where(row + low >= FIRST, 1.0, keep_lower)
        fields[step, tiles(low, 8), :] = lower.reshape(8 * SUB, LANES)
        fields[step, tiles(high, 8), :] = upper.reshape(8 * SUB, LANES)


def vertical_columns(band_ref, group_ref, out_ref):
    band = band_ref[...]
    group = group_ref[...]
    group = jnp.concatenate([group, group], axis=1)
    coefs = []
    for offset in range(-3, 4):
        coef = band[offset + 3 : offset + 4, :] + (1.0 if offset == 0 else 0.0)
        coef = jnp.concatenate([coef, coef], axis=1)
        ahead = group if offset == 0 else pltpu.roll(group, (-offset) % LANES, 1)
        coef = jnp.where(ahead == group, coef, 0.0)
        coefs.append(jnp.concatenate([coef, coef], axis=1))

    @pl.loop(0, 8)
    def _(part):
        shape = (32, 256)
        row = lax.broadcasted_iota(jnp.int32, shape, 0) + 32 * part
        col = lax.broadcasted_iota(jnp.int32, shape, 1)
        half, member, level = (row // 4) % 2, (row // 2) % 2, row % 2
        apart = 2 * (row // SUB) + level + 1024 * (2 * member + half) - col % 64 - 1024 * (col // 64)
        total = jnp.zeros(shape, F32)
        for offset in range(-3, 4):
            total = jnp.where(apart == offset, coefs[offset + 3], total)
        out_ref[pl.ds(pl.multiple_of(32 * part, 32), 32), :] = total


def two_parts(x):
    high = x.astype(jnp.bfloat16)
    return high, (x - high.astype(F32)).astype(jnp.bfloat16)


def split_matrix(matrix, out_ref):
    high, low = two_parts(matrix)
    out_ref[:, 0:256] = high
    out_ref[:, 256:512] = high
    out_ref[:, 512:768] = low


def product(matrix_ref, x):
    high, low = two_parts(x)
    return jnp.dot(matrix_ref[...], jnp.concatenate([high, low, high], axis=0), preferred_element_type=F32)


def kernel(
    control_hbm, members_hbm, east_hbm, south_hbm, innovation_hbm, huber_hbm, band_hbm, group_hbm,
    out,
    control, members, east_in, south_in, innovation, huber, band, group,
    east, west, south, fields, back_fields, east_edge, south_edge,
    gathered, lift, relay, full_matrix, lower_matrix, upper_matrix,
    term, parts, share,
    local_sems, edge_send, edge_recv, fwd_sems, sum_sems, share_sems,
    back_sems, block_sems, relay_sems, pair_sems, lev_ready, mem_ready,
):
    m, l, r = lax.axis_index("mem"), lax.axis_index("lev"), lax.axis_index("row")
    along, across = l // WIDE, lax.rem(l, WIDE)
    has_lower = (r + BLOCKS - 1) // BLOCKS
    has_upper = 1 - (r + 1) // BLOCKS
    low_edge = 1 - (l + LEVS - HALO) // LEVS
    high_edge = (l + HALO) // LEVS
    from_low = low_edge * has_lower
    from_high = high_edge * has_upper
    parity = lax.rem(r, 2)
    pair_along = 3 * (1 - parity)
    in_pair_rows = jnp.where(along == pair_along, 1, 0)
    coefs = (east, west, south)

    def leader(row):
        return 28 - 24 * (row // 2)

    is_leader = jnp.where(l == leader(r), 1, 0)
    is_root = m // ROOT

    def remote(source, target, send, recv, **where):
        return pltpu.make_async_remote_copy(
            src_ref=source, dst_ref=target, send_sem=send, recv_sem=recv,
            device_id=where, device_id_type=MESH,
        )

    barrier = pltpu.get_barrier_semaphore()

    def tell(sem, **where):
        pl.semaphore_signal(sem, inc=1, device_id=where, device_id_type=MESH)

    @pl.when(r > 0)
    def _():
        tell(barrier, row=r - 1)

    @pl.when(r < BLOCKS - 1)
    def _():
        tell(barrier, row=r + 1)

    @pl.when(is_leader == 0)
    def _():
        tell(barrier, lev=leader(r))

    @pl.when(is_root == 0)
    def _():
        tell(barrier, mem=ROOT)

    @pl.when(from_low == 1)
    def _():
        tell(barrier, lev=leader(r - 1), row=r - 1)

    @pl.when(from_high == 1)
    def _():
        tell(barrier, lev=leader(r + 1), row=r + 1)

    loads = [
        pltpu.make_async_copy(source, target, local_sems.at[i])
        for i, (source, target) in enumerate([
            (control_hbm, control), (east_hbm, east_in), (south_hbm, south_in),
            (band_hbm, band), (group_hbm, group),
            (members_hbm, members), (innovation_hbm, innovation), (huber_hbm, huber),
        ])
    ]
    for load in loads:
        load.start()

    blank = jnp.zeros((HALO * SUB, LANES), F32)
    halo_refs = (east, west, south, fields.at[0], back_fields.at[0])

    @pl.when(r == 0)
    def _():
        for ref in halo_refs:
            ref[tiles(0, HALO), :] = blank

    @pl.when(r == BLOCKS - 1)
    def _():
        for ref in halo_refs:
            ref[tiles(FIRST + LATS, HALO), :] = blank

    loads[0].wait()
    for member in range(2):
        for level in range(2):
            own = control[member, level].astype(F32)
            for half in range(2):
                fields[0, pl.ds(SUB * FIRST + sublane(member, level, half), LATS, stride=SUB), :] = own[
                    :, half * LANES : (half + 1) * LANES
                ]
    loads[1].wait()
    loads[2].wait()

    pl.semaphore_wait(
        barrier,
        has_lower + has_upper + is_root * (MEMS - 1)
        + is_leader * (LEVS - 1 + HALO * (has_lower + has_upper)),
    )

    def edge_copies(side, row):
        edge = slice(0, HALO) if side == 0 else slice(LATS - HALO, LATS)
        first = FIRST if side == 0 else FIRST + LATS - HALO
        landing = FIRST + LATS if side == 0 else 0
        return [
            remote(fields.at[0, tiles(first, HALO), :], fields.at[0, tiles(landing, HALO), :],
                   edge_send.at[side, 0], edge_recv.at[side, 0], row=row),
            remote(east_in.at[:, edge, :], east_edge.at[side],
                   edge_send.at[side, 1], edge_recv.at[side, 1], row=row),
            remote(south_in.at[:, edge, :], south_edge.at[side],
                   edge_send.at[side, 2], edge_recv.at[side, 2], row=row),
        ]

    @pl.when(r > 0)
    def _():
        for copy in edge_copies(0, r - 1):
            copy.start()

    @pl.when(r < BLOCKS - 1)
    def _():
        for copy in edge_copies(1, r + 1):
            copy.start()

    @pl.when(is_leader == 1)
    def _():
        @pl.loop(1, LEVS)
        def _(i):
            tell(lev_ready, lev=lax.rem(l + i, LEVS))

        @pl.when(r < BLOCKS - 1)
        def _():
            @pl.loop(0, HALO)
            def _(i):
                tell(lev_ready, lev=i, row=r + 1)

        @pl.when(r > 0)
        def _():
            @pl.loop(0, HALO)
            def _(i):
                tell(lev_ready, lev=LEVS - HALO + i, row=r - 1)

    @pl.when(is_root == 1)
    def _():
        @pl.loop(0, MEMS - 1)
        def _(i):
            tell(mem_ready, mem=i)

    def place(target, value, level, first, count):
        for half in range(2):
            for member in range(2):
                target[pl.ds(SUB * first + sublane(member, level, half), count, stride=SUB), :] = value[
                    :, half * LANES : (half + 1) * LANES
                ]

    def set_west(first):
        value = east[tiles(first, 8), :].reshape(8, SUB, LANES)
        west[tiles(first, 8), :] = previous_longitude(value, lane_index()).reshape(8 * SUB, LANES)

    for level in range(2):
        place(east, east_in[level], level, FIRST, LATS)
        place(south, south_in[level], level, FIRST, LATS)
    for first in range(FIRST, FIRST + LATS, 8):
        set_west(first)
    diffuse_inside(fields, coefs)

    for load in loads[3:]:
        load.wait()
    vertical_columns(band, group, full_matrix)
    split_matrix(full_matrix[...], upper_matrix)
    split_matrix(full_matrix[...].T, lower_matrix)

    pl.semaphore_wait(lev_ready, 1 - is_leader + from_low + from_high)

    def send_latitudes(rows):
        for apart in FAR_FIRST:
            for row in rows:
                peer = WIDE * row + lax.rem(across + apart, WIDE)

                def send(peer=peer):
                    remote(fields.at[PASSES, tiles(FIRST + peer, 1), :], gathered.at[tiles(l, 1), :],
                           fwd_sems.at[0], fwd_sems.at[1], lev=peer).start()

                if apart:
                    send()
                else:
                    pl.when(along != row)(send)

    send_latitudes((1, 2))

    def take_edge(side, first):
        for copy in edge_copies(side, r):
            copy.wait_recv()
        for level in range(2):
            place(east, east_edge[side, level], level, first, HALO)
            place(south, south_edge[side, level], level, first, HALO)
        set_west(first)

    @pl.when(r < BLOCKS - 1)
    def _():
        take_edge(0, FIRST + LATS)

    @pl.when(r > 0)
    def _():
        take_edge(1, 0)

    keep_lower = has_lower.astype(F32)
    diffuse_edges(fields, coefs, keep_lower)
    send_latitudes((3, 0))

    gathered[tiles(l, 1), :] = fields[PASSES, tiles(FIRST + l, 1), :]
    everyone = remote(fields.at[PASSES, tiles(FIRST, LEVS - 1), :], gathered.at[tiles(0, LEVS - 1), :],
                      fwd_sems.at[0], fwd_sems.at[1], lev=l)
    everyone.wait_recv()

    filtered = product(lower_matrix, gathered[...])

    def member_columns(member, half):
        return members[member, :, half * LANES : (half + 1) * LANES].astype(F32)

    for half in range(2):
        term[half] = sum(
            member_columns(member, half) * filtered[64 * (2 * member + half) : 64 * (2 * member + half + 1)]
            for member in range(2)
        )

    roots = (ROOT, 0)
    orders = ((0, 6, 1, 5, 2, 4, 3), (1, 7, 2, 6, 3, 5, 4))

    def term_copy(half):
        return remote(term.at[half], parts.at[m - half, half], sum_sems.at[0, half], sum_sems.at[1, half],
                      mem=roots[half])

    def share_copy(half, mem):
        return remote(share.at[half], share.at[half], share_sems.at[0, half], share_sems.at[1, half], mem=mem)

    def rest(half, sems):
        others = parts.at[pl.ds(0, MEMS - 1), half]
        return remote(others, others, sems.at[0, half], sems.at[1, half], mem=m)

    def gather_half(half):
        rest(half, sum_sems).wait_recv()
        values = [parts[i, half] for i in range(MEMS - 1)]
        values.insert(roots[half], term[half])
        increment = values[0]
        for value in values[1:]:
            increment = increment + value
        lanes = slice(half * LANES, (half + 1) * LANES)
        residual = increment - innovation[:, lanes]
        scale = HUBER / jnp.maximum(jnp.abs(residual), HUBER)
        share[half] = jnp.where(huber[:, lanes] == 1, scale, 1.0) * residual
        for mem in orders[half]:
            share_copy(half, mem).start()

    @pl.when(is_root == 0)
    def _():
        pl.semaphore_wait(mem_ready, 1)
        term_copy(0).start()

    @pl.when(m > 0)
    def _():
        term_copy(1).start()

    @pl.when(is_root == 1)
    def _():
        gather_half(0)
        share_copy(1, 0).wait_recv()

    @pl.when(m == 0)
    def _():
        gather_half(1)
        share_copy(0, 0).wait_recv()

    @pl.when((m > 0) & (is_root == 0))
    def _():
        for half in range(2):
            share_copy(half, 0).wait_recv()

    adjoint = jnp.concatenate(
        [member_columns(member, half) * share[half] for member in range(2) for half in range(2)], axis=0
    )
    lift[...] = product(upper_matrix, adjoint)

    def block_copy(side, position, row):
        return remote(lift.at[tiles(WIDE * position, WIDE), :], relay.at[side],
                      block_sems.at[side, 0], block_sems.at[side, 1],
                      lev=WIDE * position + across, row=row)

    def landing(side):
        return FIRST + LATS if side == 0 else 0

    def direct_copy(side, peer, row):
        return remote(lift.at[tiles(peer, 1), :], back_fields.at[0, tiles(landing(side) + across, 1), :],
                      block_sems.at[side, 2], relay_sems.at[side, 1], lev=peer, row=row)

    def send_edges(side, positions, row):
        for position in range(DIRECT):
            for apart in FAR_FIRST:
                direct_copy(side, WIDE * position + lax.rem(across + apart, WIDE), row).start()
        for position in positions:
            block_copy(side, position, row).start()

    @pl.when((r == 2) & (low_edge == 1))
    def _():
        send_edges(0, range(DIRECT, 4), 1)

    @pl.when((r == 1) & (high_edge == 1))
    def _():
        send_edges(1, range(3, DIRECT - 1, -1), 2)

    for apart in FAR_FIRST:
        for turn in range(4):
            if apart or turn:
                peer = WIDE * lax.rem(along + turn, 4) + lax.rem(across + apart, WIDE)
                remote(lift.at[tiles(peer, 1), :], back_fields.at[0, tiles(FIRST + l, 1), :],
                       back_sems.at[0], back_sems.at[2 - in_pair_rows], lev=peer).start()

    back_fields[0, tiles(FIRST + l, 1), :] = lift[tiles(l, 1), :]

    def hand_on(side):
        block_copy(side, along, r).wait_recv()
        for apart in FAR_FIRST[:-1]:
            column = lax.rem(across + apart, WIDE)
            remote(relay.at[side, tiles(column, 1), :],
                   back_fields.at[0, tiles(landing(side) + across, 1), :],
                   relay_sems.at[side, 0], relay_sems.at[side, 1], lev=WIDE * along + column).start()
        back_fields[0, tiles(landing(side) + across, 1), :] = relay[side, tiles(across, 1), :]

    def handed(side, count):
        return remote(relay.at[side, tiles(0, count), :],
                      back_fields.at[0, tiles(landing(side), count), :],
                      relay_sems.at[side, 0], relay_sems.at[side, 1], lev=l)

    @pl.when((r == 2) & (along >= DIRECT))
    def _():
        hand_on(1)

    @pl.when((r == 1) & (along >= DIRECT))
    def _():
        hand_on(0)

    def columns(group, count):
        return remote(lift.at[tiles(0, count), :], back_fields.at[0, tiles(FIRST, count), :],
                      back_sems.at[0], back_sems.at[group], lev=l)

    def to_pair(source, target, row):
        return remote(back_fields.at[0, tiles(source, HALO), :], back_fields.at[0, tiles(target, HALO), :],
                      pair_sems.at[0], pair_sems.at[1], row=row)

    def pair_copy(even, row):
        if even:
            return to_pair(FIRST + LATS - HALO, 0, row)
        return to_pair(FIRST, FIRST + LATS, row)

    @pl.when(in_pair_rows == 1)
    def _():
        columns(1, WIDE - 1).wait_recv()

    @pl.when(in_pair_rows == 0)
    def _():
        columns(1, WIDE).wait_recv()

    @pl.when(parity == 0)
    def _():
        pair_copy(True, r + 1).start()

    @pl.when(parity == 1)
    def _():
        pair_copy(False, r - 1).start()

    @pl.when(in_pair_rows == 1)
    def _():
        columns(2, LEVS - WIDE).wait_recv()

    @pl.when(in_pair_rows == 0)
    def _():
        columns(2, LEVS - WIDE - 1).wait_recv()

    diffuse_inside(back_fields, coefs)

    @pl.when(parity == 0)
    def _():
        pair_copy(False, r + 1).wait_recv()

    @pl.when(parity == 1)
    def _():
        pair_copy(True, r - 1).wait_recv()

    def halo_arrived(side):
        @pl.when(along >= DIRECT)
        def _():
            handed(side, WIDE - 1).wait_recv()

        @pl.when(along < DIRECT)
        def _():
            handed(side, WIDE).wait_recv()

    @pl.when(r == 2)
    def _():
        halo_arrived(1)

    @pl.when(r == 1)
    def _():
        halo_arrived(0)

    diffuse_edges(back_fields, coefs, keep_lower)

    for member in range(2):
        for level in range(2):
            for half in range(2):
                lanes = slice(half * LANES, (half + 1) * LANES)
                smooth = back_fields[
                    PASSES, pl.ds(SUB * FIRST + sublane(member, level, half), LATS, stride=SUB), :
                ]
                out[member, level, :, lanes] = control[member, level, :, lanes].astype(F32) + smooth


    @pl.when(r > 0)
    def _():
        for copy in edge_copies(0, r - 1):
            copy.wait_send()

    @pl.when(r < BLOCKS - 1)
    def _():
        for copy in edge_copies(1, r + 1):
            copy.wait_send()

    @pl.when((r == 2) & (along >= DIRECT))
    def _():
        handed(1, WIDE - 1).wait_send()

    @pl.when((r == 1) & (along >= DIRECT))
    def _():
        handed(0, WIDE - 1).wait_send()

    @pl.when(parity == 0)
    def _():
        pair_copy(True, r + 1).wait_send()

    @pl.when(parity == 1)
    def _():
        pair_copy(False, r - 1).wait_send()

    everyone.wait_send()

    @pl.when(is_root == 0)
    def _():
        term_copy(0).wait_send()

    @pl.when(m > 0)
    def _():
        term_copy(1).wait_send()

    @pl.when(is_root == 1)
    def _():
        rest(0, share_sems).wait_send()

    @pl.when(m == 0)
    def _():
        rest(1, share_sems).wait_send()

    def edges_sent(side):
        for way, count in ((0, LEVS - DIRECT * WIDE), (2, DIRECT * WIDE)):
            remote(lift.at[tiles(0, count), :], lift.at[tiles(0, count), :],
                   block_sems.at[side, way], block_sems.at[side, 1], lev=l).wait_send()

    @pl.when((r == 2) & (low_edge == 1))
    def _():
        edges_sent(0)

    @pl.when((r == 1) & (high_edge == 1))
    def _():
        edges_sent(1)

    columns(1, LEVS - 1).wait_send()


def per_device(
    control, members, east_coef, south_coef, innovation, huber_class, band, level_group_index
):
    hbm = pl.BlockSpec(memory_space=pl.ANY)
    dma = pltpu.SemaphoreType.DMA
    group = level_group_index.reshape(1, -1)
    rows = pltpu.VMEM((SUB * ROWS, LANES), F32)
    return pl.pallas_call(
        kernel,
        out_shape=jax.ShapeDtypeStruct(control.shape, F32),
        in_specs=[hbm] * 8,
        out_specs=pl.BlockSpec(memory_space=pltpu.VMEM),
        scratch_shapes=[
            pltpu.VMEM(control.shape, jnp.bfloat16),
            pltpu.VMEM(members.shape, jnp.bfloat16),
            pltpu.VMEM(east_coef.shape, F32),
            pltpu.VMEM(south_coef.shape, F32),
            pltpu.VMEM(innovation.shape, F32),
            pltpu.VMEM(huber_class.shape, jnp.int32),
            pltpu.VMEM(band.shape, F32),
            pltpu.VMEM(group.shape, jnp.int32),
            rows,
            rows,
            rows,
            pltpu.VMEM((PASSES + 1, SUB * ROWS, LANES), F32),
            pltpu.VMEM((PASSES + 1, SUB * ROWS, LANES), F32),
            pltpu.VMEM((2, 2, HALO, 2 * LANES), F32),
            pltpu.VMEM((2, 2, HALO, 2 * LANES), F32),
            pltpu.VMEM((SUB * LEVS, LANES), F32),
            pltpu.VMEM((SUB * LEVS, LANES), F32),
            pltpu.VMEM((2, SUB * WIDE, LANES), F32),
            pltpu.VMEM((256, 256), F32),
            pltpu.VMEM((256, 768), jnp.bfloat16),
            pltpu.VMEM((256, 768), jnp.bfloat16),
            pltpu.VMEM((2, 64, LANES), F32),
            pltpu.VMEM((MEMS - 1, 2, 64, LANES), F32),
            pltpu.VMEM((2, 64, LANES), F32),
            dma((8,)),
            dma((2, 3)),
            dma((2, 3)),
            dma((2,)),
            dma((2, 2)),
            dma((2, 2)),
            dma((3,)),
            dma((2, 3)),
            dma((2, 2)),
            dma((2,)),
            pltpu.SemaphoreType.REGULAR,
            pltpu.SemaphoreType.REGULAR,
        ],
        compiler_params=pltpu.CompilerParams(collective_id=0, has_side_effects=True, vmem_limit_bytes=16 << 20),
        name="hybrid_gradient",
    )(*[pltpu.with_memory_space_constraint(x, pltpu.HBM) for x in (control, members, east_coef, south_coef, innovation, huber_class, band, group)])


def solution(mesh):
    placed = (
        P("mem", "lev", "row", None),
        P("mem", None, ("row", "lev")),
        P("lev", "row", None),
        P("lev", "row", None),
        P(None, ("row", "lev")),
        P(None, ("row", "lev")),
        P(),
        P(),
    )
    return jax.shard_map(
        per_device,
        mesh=mesh,
        in_specs=placed,
        out_specs=P("mem", "lev", "row", None),
        check_vma=False,
    )
```
